256 devices in a mesh: head: 16 (over x, y), qblk: 16 (over z, core).
Axes of the slice: x: 4, y: 4, z: 8, core: 2. Of those that a mesh axis runs over, the one named last changes fastest.
Arguments:
- queries: bfloat16 [32768, 4096], P(('qblk', 'head')), may hold values from -6 to 6
- key_states: bfloat16 [32768, 1024], P(('qblk', 'head')), may hold values from -6 to 6
- value_states: bfloat16 [32768, 1024], P(('qblk', 'head')), may hold values from -6 to 6
- vertical_blocks: int32 [32, 5], replicated, may hold values from 0 to 510, as said below
- slash_offsets: int32 [32, 8], replicated, may hold values from 1 to 64, as said below
Outputs:
- attended: bfloat16 [32768, 4096], P(('qblk', 'head'))
The draws below stay inside these ranges and needn't reach their ends.
Inputs may be any that keep to these rules, and one draw needn't show every extreme that they name: `vertical_blocks`: each head names 5 distinct blocks, among them block 0 and block 510. `slash_offsets`: each head names 8 distinct offsets, among them 1 and 64.
All inputs are finite; a program needn't handle non-finite values.
Results may differ from the reference program's by a relative error of at most 0.0033.
Values may be sent and summed in bfloat16 or wider, within the bound.
No kernel may reach another device: no remote copies, remote signals or barrier semaphores. Data moves between devices by JAX's collectives and lax.ppermute only.
A program may use at most 64 MiB of HBM per device.

```python
import jax
import jax.numpy as jnp
from jax import lax

H = 32
KVH = 8
HD = 128
BLK = 64
NV = 5
NS = 8
ROWS_Q = 2048
NB_DEV = 32
SEQ = 32768
NB = 512


def drawn_pair(base_key):
    mixed = jax.random.fold_in(base_key, 7)
    key_list = jax.random.split(mixed, 4)
    query_vals = jnp.clip(1.5 * jax.random.normal(key_list[1], (SEQ, H * HD), jnp.float32), -6.0, 6.0)
    key_vals = jnp.clip(1.5 * jax.random.normal(key_list[3], (SEQ, KVH * HD), jnp.float32), -6.0, 6.0)
    return (query_vals.astype(jnp.float32), key_vals.astype(jnp.float32))


def draw_queries(key, part):
    return drawn_pair(key)[0].astype(jnp.bfloat16)


def draw_key_states(key, part):
    return drawn_pair(key)[1].astype(jnp.bfloat16)


def draw_vertical_blocks(key, part):
    head_keys = jax.random.split(jax.random.fold_in(key, 11), H)

    def pick_middle(head_key):
        return jax.random.permutation(head_key, NB - 3)[:NV - 2] + 1
    middle = jax.vmap(pick_middle)(head_keys).astype(jnp.int32)
    first_col = jnp.zeros((H, 1), jnp.int32)
    last_col = jnp.full((H, 1), NB - 2, jnp.int32)
    return jnp.concatenate([first_col, last_col, middle], axis=1)


def draw_slash_offsets(key, part):
    head_keys = jax.random.split(jax.random.fold_in(key, 13), H)

    def pick_middle(head_key):
        return jax.random.permutation(head_key, 2 * NB_DEV - 2)[:NS - 2] + 2
    middle = jax.vmap(pick_middle)(head_keys).astype(jnp.int32)
    first_col = jnp.ones((H, 1), jnp.int32)
    last_col = jnp.full((H, 1), 2 * NB_DEV, jnp.int32)
    return jnp.concatenate([first_col, last_col, middle], axis=1)


def block_levels(own_key, shape, pieces, least, largest):
    loudness, own = 1.0, jax.random.fold_in(own_key, 6)
    for position, parts in pieces:
        heights = jnp.exp(jax.random.uniform(jax.random.fold_in(own, position), (parts,), jnp.float32, least / len(pieces), largest / len(pieces)))
        loudness = loudness * jnp.repeat(heights, shape[position] // parts).reshape([-1 if axis == position else 1 for axis in range(len(shape))])
    return loudness


def scatter_about(stream_key, dims, deviation, reach, pieces=(), kind=jnp.bfloat16):
    result = jax.random.normal(stream_key, dims, jnp.float32) * deviation
    if len(pieces) > 0:
        result = block_levels(stream_key, dims, pieces, -0.22, 0.18) * result
    return jnp.clip(result, min=-reach, max=reach).astype(kind)


def setup_inputs(seed: int = 0) -> dict:
    splits = jax.random.split(jax.random.key(seed), 6)
    queries = draw_queries(jax.random.fold_in(splits[5], 71), 0)
    key_states = draw_key_states(jax.random.fold_in(splits[5], 71), 0)
    value_states = scatter_about(splits[2], (SEQ, KVH * HD), 1.0, 6.0, ((0, 256),))
    vertical_blocks = draw_vertical_blocks(jax.random.fold_in(splits[5], 71), 0)
    slash_offsets = draw_slash_offsets(jax.random.fold_in(splits[5], 71), 0)
    return dict(queries=queries, key_states=key_states, value_states=value_states, vertical_blocks=vertical_blocks, slash_offsets=slash_offsets)


def attend_group(query_block_list, diagonal_key_block, diagonal_value_block, slash_key_block, slash_value_block, vertical_key_block, vertical_value_block, block_ids, slash_row, vert_row):
    number_format = jnp.float32
    logit_scale = HD ** -0.5
    query_wide_rows = query_block_list.astype(number_format)
    diagonal_scores = jnp.einsum("pwr,pgr->pwg", query_wide_rows, diagonal_key_block.astype(number_format)) * logit_scale
    slash_scores = jnp.einsum("pzf,opwf->pzow", query_wide_rows, slash_key_block.astype(number_format)) * logit_scale
    vertical_scores = jnp.einsum("ihx,zsx->ihzs", query_wide_rows, vertical_key_block.astype(number_format)) * logit_scale
    causal = jnp.arange(BLK)[:, None] >= jnp.arange(BLK)[None, :]
    diagonal_scores = jnp.where(causal[None], diagonal_scores, -jnp.inf)
    slash_ok = (block_ids[:, None] - slash_row[None, :]) >= 0
    slash_scores = jnp.where(slash_ok[:, None, :, None], slash_scores, -jnp.inf)
    block_gap = block_ids[:, None] - vert_row[None, :]
    slash_hit = jnp.any(block_gap[:, :, None] == slash_row[None, None, :], axis=2)
    vert_ok = (block_gap > 0) & jnp.logical_not(slash_hit)
    vertical_scores = jnp.where(vert_ok[:, None, :, None], vertical_scores, -jnp.inf)
    row_max = jnp.maximum(jnp.max(diagonal_scores, axis=2), jnp.maximum(jnp.max(slash_scores, axis=(2, 3)), jnp.max(vertical_scores, axis=(2, 3))))
    diagonal_weights = jnp.exp(diagonal_scores - row_max[:, :, None])
    slash_weights = jnp.exp(slash_scores - row_max[:, :, None, None])
    vertical_weights = jnp.exp(vertical_scores - row_max[:, :, None, None])
    row_total = jnp.sum(diagonal_weights, axis=2) + jnp.sum(slash_weights, axis=(2, 3)) + jnp.sum(vertical_weights, axis=(2, 3))
    diagonal_row_max = lax.optimization_barrier(diagonal_weights.astype(jnp.bfloat16)).astype(number_format)
    slash_row_max = lax.optimization_barrier(slash_weights.astype(jnp.bfloat16)).astype(number_format)
    vertical_row_max = lax.optimization_barrier(vertical_weights.astype(jnp.bfloat16)).astype(number_format)
    weight_total = jnp.einsum("rmt,rtl->rml", diagonal_row_max, diagonal_value_block.astype(number_format))
    weight_total = weight_total + jnp.einsum("mnop,ompj->mnj", slash_row_max, slash_value_block.astype(number_format))
    weight_total = weight_total + jnp.einsum("tiyx,yxf->tif", vertical_row_max, vertical_value_block.astype(number_format))
    return (weight_total / row_total[:, :, None]).astype(jnp.bfloat16)


def reference(queries, key_states, value_states, vertical_blocks, slash_offsets):
    group_rows = min(512, ROWS_Q)
    group_blocks = group_rows // BLK
    front = 2 * ROWS_Q
    ratio_heads = H // KVH

    def one_head(head_id):
        kv_head = head_id // ratio_heads
        q_head = lax.dynamic_slice_in_dim(queries, head_id * HD, HD, 1)
        k_head = lax.dynamic_slice_in_dim(key_states, kv_head * HD, HD, 1)
        v_head = lax.dynamic_slice_in_dim(value_states, kv_head * HD, HD, 1)
        slash_row = slash_offsets[head_id]
        vert_row = vertical_blocks[head_id]
        k_padded = jnp.concatenate([jnp.zeros((front, HD), k_head.dtype), k_head], axis=0)
        v_padded = jnp.concatenate([jnp.zeros((front, HD), v_head.dtype), v_head], axis=0)
        vertical_key_block = k_head.reshape(NB, BLK, HD)[vert_row]
        vertical_value_block = v_head.reshape(NB, BLK, HD)[vert_row]

        def one_group(group_index):
            start_row = (group_index * group_rows).astype(jnp.int32)
            query_block_list = lax.dynamic_slice_in_dim(q_head, start_row, group_rows, 0).reshape(group_blocks, BLK, HD)
            diagonal_key_block = lax.dynamic_slice_in_dim(k_head, start_row, group_rows, 0).reshape(group_blocks, BLK, HD)
            diagonal_value_block = lax.dynamic_slice_in_dim(v_head, start_row, group_rows, 0).reshape(group_blocks, BLK, HD)

            def slash_rows(padded, offset_blocks):
                return lax.dynamic_slice_in_dim(padded, (start_row + front - offset_blocks * BLK).astype(jnp.int32), group_rows, 0)

            slash_key_block = jax.vmap(slash_rows, in_axes=(None, 0))(k_padded, slash_row).reshape(NS, group_blocks, BLK, HD)
            slash_value_block = jax.vmap(slash_rows, in_axes=(None, 0))(v_padded, slash_row).reshape(NS, group_blocks, BLK, HD)
            block_ids = (start_row // BLK + jnp.arange(group_blocks, dtype=jnp.int32)).astype(jnp.int32)
            return attend_group(query_block_list, diagonal_key_block, diagonal_value_block, slash_key_block, slash_value_block, vertical_key_block, vertical_value_block, block_ids, slash_row, vert_row)

        outputs = lax.map(one_group, jnp.arange(SEQ // group_rows, dtype=jnp.int32))
        return outputs.reshape(SEQ, HD)

    heads = lax.map(one_head, jnp.arange(H, dtype=jnp.int32))
    return jnp.transpose(heads, (1, 0, 2)).reshape(SEQ, H * HD)
```

```python
import functools

import jax
import jax.numpy as jnp
from jax import lax
from jax.experimental import pallas as pl
from jax.experimental.pallas import tpu as pltpu
from jax.sharding import PartitionSpec as P

H = 32
KVH = 8
HD = 128
BLK = 64
NV = 5
NS = 8
NBD = 32
RUN = 4096
NSLOT = 10
LOG2E = 1.4426950408889634


def attn_kernel(QB, UNROLL, off_ref, bias_ref, par_ref, q_ref, own, swp, pas, sh2, vert, o_ref, kvs, sem):
    step = pl.program_id(0)

    @pl.when(step == 0)
    def _():
        odd = par_ref[0] == 1
        c0 = pltpu.make_async_copy(sh2, kvs.at[pl.ds(0, RUN)], sem.at[0])
        c2 = pltpu.make_async_copy(own, kvs.at[pl.ds(2 * RUN, RUN)], sem.at[2])
        c3 = pltpu.make_async_copy(vert, kvs.at[pl.ds(3 * RUN, vert.shape[0])], sem.at[3])
        c0.start()
        c2.start()
        c3.start()

        @pl.when(odd)
        def _():
            c1 = pltpu.make_async_copy(swp, kvs.at[pl.ds(RUN, RUN)], sem.at[1])
            c1.start()
            c1.wait()

        @pl.when(jnp.logical_not(odd))
        def _():
            c1 = pltpu.make_async_copy(pas, kvs.at[pl.ds(RUN, RUN)], sem.at[1])
            c1.start()
            c1.wait()

        c0.wait()
        c2.wait()
        c3.wait()

    lane = lax.broadcasted_iota(jnp.int32, (1, 128), 1)
    rr = lax.broadcasted_iota(jnp.int32, (BLK, 128), 0)
    cc = lax.broadcasted_iota(jnp.int32, (BLK, 128), 1)
    causal = (rr >= cc) | (cc >= BLK)
    scale = (HD**-0.5) * LOG2E

    def one(il, hh):
        base = (hh * NBD + step * QB + il) * 16
        row = pl.multiple_of(il * BLK, BLK)
        offs = [pl.multiple_of(off_ref[base + n], BLK) for n in range(14)]
        q = q_ref[pl.ds(row, BLK), hh * HD : (hh + 1) * HD]
        k = jnp.concatenate([kvs[pl.ds(o, BLK), :] for o in offs], axis=0)
        s = lax.dot_general(q, k, (((1,), (1,)), ((), ())), preferred_element_type=jnp.float32)
        parts = []
        for c in range(7):
            b = jnp.where(lane < BLK, bias_ref[base + 2 * c], bias_ref[base + 2 * c + 1])
            x = s[:, c * 128 : (c + 1) * 128] + b
            if c == 0:
                x = jnp.where(causal, x, -jnp.inf)
            parts.append(x)
        m = jnp.max(functools.reduce(jnp.maximum, parts), axis=1, keepdims=True)
        ps = [jnp.exp2((x - m) * scale) for x in parts]
        total = jnp.sum(functools.reduce(jnp.add, ps), axis=1, keepdims=True)
        p = jnp.concatenate([x.astype(jnp.bfloat16) for x in ps], axis=1)
        v = jnp.concatenate([kvs[pl.ds(o + 128, BLK), :] for o in offs], axis=0)
        acc = jnp.dot(p, v, preferred_element_type=jnp.float32)
        o_ref[pl.ds(row, BLK), hh * HD : (hh + 1) * HD] = (acc / total).astype(o_ref.dtype)

    def body(t, carry):
        for u in range(UNROLL):
            for hh in range(2):
                one(t * UNROLL + u, hh)
        return carry

    lax.fori_loop(0, QB // UNROLL, body, 0)


def attend(off, bias, par, q, own, swp, pas, sh2, vert, QB=8, UNROLL=2):
    hbm = pl.BlockSpec(memory_space=pl.ANY)
    smem = pl.BlockSpec(memory_space=pltpu.SMEM)
    tile = pl.BlockSpec((QB * BLK, 2 * HD), lambda i: (i, 0))
    return pl.pallas_call(
        functools.partial(attn_kernel, QB, UNROLL),
        grid=(NBD // QB,),
        out_shape=jax.ShapeDtypeStruct((NBD * BLK, 2 * HD), jnp.bfloat16),
        in_specs=[smem, smem, smem, tile, hbm, hbm, hbm, hbm, hbm],
        out_specs=tile,
        scratch_shapes=[
            pltpu.VMEM((3 * RUN + vert.shape[0], HD), jnp.bfloat16),
            pltpu.SemaphoreType.DMA((4,)),
        ],
        cost_estimate=pl.CostEstimate(flops=2_000_000_000, bytes_accessed=6_000_000, transcendentals=4_000_000),
        name="attend",
    )(off, bias, par, q, own, swp, pas, sh2, vert)


def pick_kernel(src_ref, ok_ref, kv_ref, o_ref):
    for n in range(NSLOT):
        src = pl.multiple_of(src_ref[n], BLK)
        ok = jnp.full((BLK, HD), ok_ref[n], jnp.int32) == 1
        dst = (n // 2) * 256 + (n % 2) * BLK
        for part in range(2):
            x = kv_ref[pl.ds(src + 128 * part, BLK), :].astype(jnp.float32)
            o_ref[dst + 128 * part : dst + 128 * part + BLK, :] = jnp.where(ok, x, 0.0).astype(jnp.bfloat16)


def pick(src, ok, kv):
    smem = pl.BlockSpec(memory_space=pltpu.SMEM)
    vmem = pl.BlockSpec(memory_space=pltpu.VMEM)
    return pl.pallas_call(
        pick_kernel,
        out_shape=jax.ShapeDtypeStruct((NSLOT * 128, HD), jnp.bfloat16),
        in_specs=[smem, smem, vmem],
        out_specs=vmem,
        cost_estimate=pl.CostEstimate(flops=1_000_000, bytes_accessed=1_500_000, transcendentals=0),
        name="pick",
    )(src, ok, kv)


def place(block):
    return (block // 2) * 256 + (block % 2) * BLK


def tables(vertical_blocks, slash_offsets, head, run):
    vert = lax.dynamic_slice_in_dim(vertical_blocks, head * 2, 2, 0)
    slash = lax.dynamic_slice_in_dim(slash_offsets, head * 2, 2, 0)
    il = jnp.arange(NBD, dtype=jnp.int32)
    i = run * NBD + il
    zero = jnp.zeros((2, NBD, 1), jnp.int32)
    back = jnp.concatenate([zero, jnp.broadcast_to(slash[:, None, :], (2, NBD, NS))], axis=2)
    slot = jnp.arange(NSLOT, dtype=jnp.int32).reshape(2, 1, NV)
    off_window = place(2 * NBD + il[None, :, None] - back)
    off_vert = jnp.broadcast_to(3 * RUN + place(slot), (2, NBD, NV))
    off = jnp.concatenate([off_window, off_vert, zero, zero], axis=2).reshape(-1)
    gap = i[None, :, None] - vert[:, None, :]
    hit = jnp.any(gap[:, :, :, None] == slash[:, None, None, :], axis=3)
    ok_vert = (gap > 0) & jnp.logical_not(hit)
    ok_window = i[None, :, None] - back >= 0
    ok = jnp.concatenate([ok_window, ok_vert, zero == 0, zero == 0], axis=2).reshape(-1)
    bias = jnp.where(ok, 0.0, -jnp.inf).astype(jnp.float32)
    local = vert.reshape(-1) - run * NBD
    mine = (local >= 0) & (local < NBD)
    src = place(jnp.clip(local, 0, NBD - 1))
    return off, bias, src, mine.astype(jnp.int32)


def per_device(queries, key_states, value_states, vertical_blocks, slash_offsets):
    head = lax.axis_index("head")
    run = lax.axis_index("qblk")
    rows = queries.shape[0]
    runs = lax.axis_size("qblk")
    off, bias, src, mine = tables(vertical_blocks, slash_offsets, head, run)
    k3 = key_states.reshape(rows, KVH, HD).transpose(1, 0, 2)
    v3 = value_states.reshape(rows, KVH, HD).transpose(1, 0, 2)
    kv = jnp.repeat(jnp.stack([k3, v3], axis=1), 2, axis=0)
    own = lax.all_to_all(kv, "head", split_axis=0, concat_axis=0, tiled=True).reshape(RUN, HD)
    swap = [(r, r ^ 1) for r in range(runs)]
    sh2 = lax.ppermute(own, "qblk", [(r, (r + 2) % runs) for r in range(runs)])
    swp = lax.ppermute(own, "qblk", swap)
    pas = lax.ppermute(sh2, "qblk", swap)
    cand = pick(src, mine, own).reshape(runs, NSLOT * 128 // runs, HD)
    cand = lax.all_to_all(cand, "qblk", split_axis=0, concat_axis=0, tiled=True)
    mine_part = jnp.sum(cand.astype(jnp.float32), axis=0).astype(jnp.bfloat16)
    vert = lax.all_gather(mine_part, "qblk", axis=0, tiled=True)
    q = lax.all_to_all(queries, "head", split_axis=1, concat_axis=0, tiled=True)
    par = (run % 2).astype(jnp.int32).reshape(1)
    out = attend(off, bias, par, q, own, swp, pas, sh2, vert)
    return lax.all_to_all(out, "head", split_axis=0, concat_axis=1, tiled=True)


def solution(mesh):
    spec = P(("qblk", "head"), None)
    return jax.shard_map(
        per_device,
        mesh=mesh,
        in_specs=(spec, spec, spec, P(), P()),
        out_specs=spec,
        check_vma=False,
    )
```

```python
import functools

import jax
import jax.numpy as jnp
from jax import lax
from jax.experimental import pallas as pl
from jax.experimental.pallas import tpu as pltpu
from jax.sharding import PartitionSpec as P

H = 32
KVH = 8
HD = 128
BLK = 64
NV = 5
NS = 8
NBD = 32
RUN = 4096
NSLOT = 10
LOG2E = 1.4426950408889634


SCALE = (HD**-0.5) * LOG2E
SIDE = 4
G = 4


def window_kernel(
    slash_ref, qa, qb, qc, qd, own, swp, pas, sh2, acc_ref, ml_ref, q_ref, kvs, s0, s1, m0, m1, sem, qsem
):
    run = lax.axis_index("qblk")
    head = lax.axis_index("head")
    head0 = 2 * head
    x = head // SIDE
    y = lax.rem(head, SIDE)
    loads = []
    for s, piece in enumerate((qa, qb, qc, qd)):
        for r in range(SIDE):
            sender = lax.rem(x + SIDE - s, SIDE) * SIDE + lax.rem(y + SIDE - r, SIDE)
            at = pl.multiple_of(sender * 128, 128)
            loads.append(pltpu.make_async_copy(piece.at[r], q_ref.at[pl.ds(at, 128)], qsem.at[s, r]))
    for load in loads:
        load.start()
    odd = lax.rem(run, 2) == 1
    c0 = pltpu.make_async_copy(sh2, kvs.at[pl.ds(0, RUN)], sem.at[0])
    c2 = pltpu.make_async_copy(own, kvs.at[pl.ds(2 * RUN, RUN)], sem.at[2])
    c0.start()
    c2.start()

    @pl.when(odd)
    def _():
        c1 = pltpu.make_async_copy(swp, kvs.at[pl.ds(RUN, RUN)], sem.at[1])
        c1.start()
        c1.wait()

    @pl.when(jnp.logical_not(odd))
    def _():
        c1 = pltpu.make_async_copy(pas, kvs.at[pl.ds(RUN, RUN)], sem.at[1])
        c1.start()
        c1.wait()

    c0.wait()
    c2.wait()
    for load in loads:
        load.wait()

    lane = lax.broadcasted_iota(jnp.int32, (1, 128), 1)
    rr = lax.broadcasted_iota(jnp.int32, (BLK, 128), 0)
    cc = lax.broadcasted_iota(jnp.int32, (BLK, 128), 1)
    causal = (rr >= cc) | (cc >= BLK)
    low = cc < BLK
    scores = (s0, s1)
    maxima = (m0, m1)

    def backs(hh):
        return [0] + [slash_ref[head0 + hh, n] for n in range(NS)]

    def offset(block):
        return pl.multiple_of((block // 2) * 256 + lax.rem(block, 2) * BLK, BLK)

    def first(t, buf):
        for g in range(G):
            il = t * (G // 2) + g // 2
            hh = g % 2
            back = backs(hh)
            i = run * NBD + il
            row = pl.multiple_of(il * BLK, BLK)
            q = q_ref[pl.ds(row, BLK), hh * HD : (hh + 1) * HD]
            m = None
            for c in range(5):
                pair = back[2 * c : 2 * c + 2]
                k = jnp.concatenate([kvs[pl.ds(offset(2 * NBD + il - s), BLK), :] for s in pair], axis=0)
                x = lax.dot_general(q, k, (((1,), (1,)), ((), ())), preferred_element_type=jnp.float32)
                width = BLK * len(pair)
                span = pair[0] if len(pair) == 1 else jnp.where(lane < BLK, pair[0], pair[1])
                ok = jnp.broadcast_to(i - span, (1, width)) >= 0
                x = x + jnp.where(ok, 0.0, -jnp.inf)
                if c == 0:
                    x = jnp.where(causal, x, -jnp.inf)
                scores[buf][g, :, c * 128 : c * 128 + width] = x
                if c < 4:
                    m = x if m is None else jnp.maximum(m, x)
                else:
                    last = jnp.max(x, axis=1, keepdims=True)
            m = jnp.maximum(jnp.max(m, axis=1, keepdims=True), last)
            maxima[buf][g] = jnp.broadcast_to(m, (BLK, 128))

    def second(t, buf):
        for g in range(G):
            il = t * (G // 2) + g // 2
            hh = g % 2
            back = backs(hh)
            row = pl.multiple_of(il * BLK, BLK)
            m = maxima[buf][g]
            total = None
            ps = []
            for c in range(5):
                width = 128 if c < 4 else BLK
                p = jnp.exp2((scores[buf][g, :, c * 128 : c * 128 + width] - m[:, :width]) * SCALE)
                ps.append(p.astype(jnp.bfloat16))
                if c < 4:
                    total = p if total is None else total + p
                else:
                    last = jnp.sum(p, axis=1, keepdims=True)
            v = jnp.concatenate([kvs[pl.ds(offset(2 * NBD + il - s) + 128, BLK), :] for s in back], axis=0)
            acc = jnp.dot(jnp.concatenate(ps, axis=1), v, preferred_element_type=jnp.float32)
            total = jnp.sum(total, axis=1, keepdims=True) + last
            acc_ref[pl.ds(row, BLK), hh * HD : (hh + 1) * HD] = acc
            ml_ref[pl.ds(row, BLK), hh * HD : (hh + 1) * HD] = jnp.where(low, m, total)

    steps = 2 * NBD // G
    first(0, 0)

    def body(u, carry):
        t = 2 * u
        first(t + 1, 1)
        second(t, 0)
        first(jnp.minimum(t + 2, steps - 1), 0)
        second(t + 1, 1)
        return carry

    lax.fori_loop(0, steps // 2, body, 0)


def window_part(slash, pieces, own, swp, pas, sh2):
    hbm = pl.BlockSpec(memory_space=pl.ANY)
    smem = pl.BlockSpec(memory_space=pltpu.SMEM)
    vmem = pl.BlockSpec(memory_space=pltpu.VMEM)
    state = jax.ShapeDtypeStruct((NBD * BLK, 2 * HD), jnp.float32)
    return pl.pallas_call(
        window_kernel,
        out_shape=(state, state, jax.ShapeDtypeStruct((NBD * BLK, 2 * HD), jnp.bfloat16)),
        in_specs=[smem] + [hbm] * 8,
        out_specs=(vmem, vmem, vmem),
        scratch_shapes=[
            pltpu.VMEM((3 * RUN, HD), jnp.bfloat16),
            pltpu.VMEM((G, BLK, 640), jnp.float32),
            pltpu.VMEM((G, BLK, 640), jnp.float32),
            pltpu.VMEM((G, BLK, 128), jnp.float32),
            pltpu.VMEM((G, BLK, 128), jnp.float32),
            pltpu.SemaphoreType.DMA((3,)),
            pltpu.SemaphoreType.DMA((SIDE, SIDE)),
        ],
        cost_estimate=pl.CostEstimate(flops=1_500_000_000, bytes_accessed=10_000_000, transcendentals=3_000_000),
        name="window_part",
    )(slash, *pieces, own, swp, pas, sh2)


TILE = 2
STEP = 8


def vertical_kernel(vert_ref, slash_ref, q_ref, acc_ref, ml_ref, kv_ref, o_ref):
    run = lax.axis_index("qblk")
    head0 = 2 * lax.axis_index("head")
    lane = lax.broadcasted_iota(jnp.int32, (1, 128), 1)
    block0 = run * NBD + pl.program_id(0) * STEP

    def body(t, carry):
        row = pl.multiple_of(t * TILE * BLK, TILE * BLK)
        rows = pl.ds(row, TILE * BLK)
        for hh in range(2):
            vs = [vert_ref[head0 + hh, n] for n in range(NV)]
            ss = [slash_ref[head0 + hh, n] for n in range(NS)]
            q = q_ref[rows, hh * HD : (hh + 1) * HD]
            base = hh * 2 * NV * BLK
            xs = []
            for c in range(3):
                pair = vs[2 * c : 2 * c + 2]
                width = BLK * len(pair)
                k = kv_ref[base + c * 128 : base + c * 128 + width, :]
                x = lax.dot_general(q, k, (((1,), (1,)), ((), ())), preferred_element_type=jnp.float32)
                v = pair[0] if len(pair) == 1 else jnp.where(lane < BLK, pair[0], pair[1])
                masks = []
                for u in range(TILE):
                    gap = jnp.broadcast_to(block0 + t * TILE + u - v, (1, width))
                    bad = gap <= 0
                    for s in ss:
                        bad = bad | (gap == s)
                    masks.append(jnp.broadcast_to(jnp.where(bad, -jnp.inf, 0.0), (BLK, width)))
                xs.append(x + jnp.concatenate(masks, axis=0))
            ml = ml_ref[rows, hh * HD : (hh + 1) * HD]
            m_old = ml[:, 0:1]
            total = ml[:, BLK : BLK + 1]
            m = jnp.max(jnp.maximum(xs[0], xs[1]), axis=1, keepdims=True)
            m = jnp.maximum(jnp.maximum(m, jnp.max(xs[2], axis=1, keepdims=True)), m_old)
            keep = jnp.exp2((m_old - m) * SCALE)
            ps = [jnp.exp2((x - m) * SCALE) for x in xs]
            total = total * keep + jnp.sum(ps[0] + ps[1], axis=1, keepdims=True) + jnp.sum(ps[2], axis=1, keepdims=True)
            p = jnp.concatenate([x.astype(jnp.bfloat16) for x in ps], axis=1)
            v = kv_ref[base + NV * BLK : base + 2 * NV * BLK, :]
            acc = acc_ref[rows, hh * HD : (hh + 1) * HD] * keep + jnp.dot(p, v, preferred_element_type=jnp.float32)
            o_ref[rows, hh * HD : (hh + 1) * HD] = (acc / total).astype(o_ref.dtype)
        return carry

    lax.fori_loop(0, STEP // TILE, body, 0, unroll=2)


def vertical_part(vert_blocks, slash, q, acc, ml, kv):
    smem = pl.BlockSpec(memory_space=pltpu.SMEM)
    vmem = pl.BlockSpec(memory_space=pltpu.VMEM)
    tile = pl.BlockSpec((STEP * BLK, 2 * HD), lambda i: (i, 0))
    return pl.pallas_call(
        vertical_kernel,
        out_shape=jax.ShapeDtypeStruct((NBD * BLK, 2 * HD), jnp.bfloat16),
        grid=(NBD // STEP,),
        in_specs=[smem, smem, tile, tile, tile, vmem],
        out_specs=tile,
        cost_estimate=pl.CostEstimate(flops=800_000_000, bytes_accessed=7_000_000, transcendentals=1_500_000),
        name="vertical_part",
    )(vert_blocks, slash, q, acc, ml, kv)


def pick_kernel(vert_ref, kv_ref, o_ref):
    run = lax.axis_index("qblk")
    head0 = 2 * lax.axis_index("head")
    for hh in range(2):
        for n in range(NV):
            local = vert_ref[head0 + hh, n] - run * NBD
            at = jnp.clip(local, 0, NBD - 1)
            src = pl.multiple_of((at // 2) * 256 + lax.rem(at, 2) * BLK, BLK)
            ok = jnp.full((BLK, HD), jnp.where(local == at, 1, 0), jnp.int32) == 1
            for part in range(2):
                x = kv_ref[pl.ds(src + 128 * part, BLK), :].astype(jnp.float32)
                dst = ((hh * 2 + part) * NV + n) * BLK
                o_ref[dst : dst + BLK, :] = jnp.where(ok, x, 0.0).astype(jnp.bfloat16)


def pick(vert_blocks, kv):
    smem = pl.BlockSpec(memory_space=pltpu.SMEM)
    vmem = pl.BlockSpec(memory_space=pltpu.VMEM)
    return pl.pallas_call(
        pick_kernel,
        out_shape=jax.ShapeDtypeStruct((NSLOT * 128, HD), jnp.bfloat16),
        in_specs=[smem, vmem],
        out_specs=vmem,
        cost_estimate=pl.CostEstimate(flops=1_000_000, bytes_accessed=1_500_000, transcendentals=0),
        name="pick",
    )(vert_blocks, kv)


def by_head(k, v):
    rows = k.shape[0]
    k3 = k.reshape(rows, KVH, HD).transpose(1, 0, 2)
    v3 = v.reshape(rows, KVH, HD).transpose(1, 0, 2)
    return jnp.repeat(jnp.stack([k3, v3], axis=1), 2, axis=0)


def exchange(x, axis):
    return lax.all_to_all(x, axis, split_axis=0, concat_axis=0, tiled=True)


def split_kernel(q_ref, *outs):
    y = lax.rem(lax.axis_index("head"), SIDE)
    for s, out in enumerate(outs):
        to = lax.rem(y + s, SIDE)
        for x in range(SIDE):
            out[x] = q_ref[:, pl.ds(pl.multiple_of((x * SIDE + to) * 256, 256), 256)]


def mix_kernel(*refs):
    x = lax.axis_index("head") // SIDE
    for s in range(SIDE):
        to = lax.rem(x + s, SIDE)
        for r in range(SIDE):
            refs[SIDE + s][r] = refs[r][to]


def four(kernel, name, *args):
    vmem = pl.BlockSpec(memory_space=pltpu.VMEM)
    piece = jax.ShapeDtypeStruct((SIDE, 128, 256), jnp.bfloat16)
    return pl.pallas_call(
        kernel,
        out_shape=(piece,) * SIDE,
        in_specs=[vmem] * len(args),
        out_specs=(vmem,) * SIDE,
        cost_estimate=pl.CostEstimate(flops=0, bytes_accessed=2_000_000, transcendentals=0),
        name=name,
    )(*args)


def send_queries(queries):
    pieces = four(split_kernel, "split_q", queries)
    across = lambda s: [(h, h // SIDE * SIDE + (h + s) % SIDE) for h in range(SIDE * SIDE)]
    pieces = [pieces[0]] + [lax.ppermute(pieces[s], "head", across(s)) for s in range(1, SIDE)]
    pieces = four(mix_kernel, "mix_q", *pieces)
    along = lambda s: [(h, (h + s * SIDE) % (SIDE * SIDE)) for h in range(SIDE * SIDE)]
    return [pieces[0]] + [lax.ppermute(pieces[s], "head", along(s)) for s in range(1, SIDE)]


def per_device(queries, key_states, value_states, vertical_blocks, slash_offsets):
    runs = lax.axis_size("qblk")
    ahead = [(r, (r + 2) % runs) for r in range(runs)]
    swap = [(r, r ^ 1) for r in range(runs)]
    own = exchange(by_head(key_states, value_states), "head").reshape(RUN, HD)
    cand = pick(vertical_blocks, own).reshape(runs, NSLOT * 128 // runs, HD)
    cand = exchange(cand, "qblk")
    sh2 = lax.ppermute(own, "qblk", ahead)
    swp = lax.ppermute(own, "qblk", swap)
    pas = lax.ppermute(sh2, "qblk", swap)
    part = jnp.sum(cand.astype(jnp.float32), axis=0).astype(jnp.bfloat16)
    vert = exchange(jnp.broadcast_to(part[None], cand.shape), "qblk").reshape(NSLOT * 128, HD)
    pieces = send_queries(queries)
    acc, ml, q = window_part(slash_offsets, pieces, own, swp, pas, sh2)
    out = vertical_part(vertical_blocks, slash_offsets, q, acc, ml, vert)
    return lax.all_to_all(out, "head", split_axis=0, concat_axis=1, tiled=True)


def solution(mesh):
    spec = P(("qblk", "head"), None)
    return jax.shard_map(
        per_device,
        mesh=mesh,
        in_specs=(spec, spec, spec, P(), P()),
        out_specs=spec,
        check_vma=False,
    )
```

```python
import jax
import jax.numpy as jnp
from jax import lax
from jax.experimental import pallas as pl
from jax.experimental.pallas import tpu as pltpu
from jax.sharding import PartitionSpec as P


KVH = 8
HD = 128
BLK = 64
NV = 5
NS = 8
NBD = 32
NSLOT = 10
LOG2E = 1.4426950408889634


SCALE = (HD**-0.5) * LOG2E
WROWS = 3 * 2048
G = 4
CH = 2


def attn_kernel(
    tab, q_in, own, swp, pas, sh2, vkv, o_ref, q_ref, ks, vs, bias, s0, s1, m0, m1, p0, p1, l0, l1, sem, sem1
):
    run = tab[0]
    odd = (run & 1) == 1
    copies = [pltpu.make_async_copy(q_in, q_ref, sem.at[0])]
    for n, part in enumerate((ks, vs)):
        for m, src in ((0, sh2), (2, own)):
            copies.append(
                pltpu.make_async_copy(src.at[:, n], part.at[pl.ds(m * 16, 16)], sem.at[1 + 2 * n + m // 2])
            )
        copies.append(pltpu.make_async_copy(vkv.at[n], part.at[pl.ds(48, 5)], sem.at[5 + n]))
    for c in copies:
        c.start()
    for cond, src in ((odd, swp), (jnp.logical_not(odd), pas)):

        @pl.when(cond)
        def _():
            both = [
                pltpu.make_async_copy(src.at[:, n], part.at[pl.ds(16, 16)], sem1.at[n])
                for n, part in enumerate((ks, vs))
            ]
            for c in both:
                c.start()
            for c in both:
                c.wait()

    lane = lax.broadcasted_iota(jnp.int32, (8, 128), 1)
    slash = [[tab[11 + hh * NS + n] for n in range(NS)] for hh in range(2)]
    vert = [[tab[1 + hh * NV + n] for n in range(NV)] for hh in range(2)]
    spans = []
    for hh in range(2):
        named = [0] + slash[hh] + vert[hh]
        spans.append([jnp.where(lane < BLK, named[2 * c], named[2 * c + 1]) for c in range(7)])

    def mask(il, carry):
        for hh in range(2):
            for c in range(7):
                gap = run * NBD + il - spans[hh][c]
                bad = gap < 0
                if c >= 4:
                    hit = gap == 0
                    for s in slash[hh]:
                        hit = hit | (gap == s)
                    if c == 4:
                        hit = hit & (lane >= BLK)
                    bad = bad | hit
                bias[2 * il + hh, :, c * 128 : (c + 1) * 128] = jnp.where(bad, -jnp.inf, 0.0)
        return carry

    lax.fori_loop(0, NBD, mask, 0, unroll=4)
    for c in copies:
        c.wait()

    rr = lax.broadcasted_iota(jnp.int32, (BLK, 128), 0)
    cc = lax.broadcasted_iota(jnp.int32, (BLK, 128), 1)
    causal = (rr >= cc) | (cc >= BLK)
    scores = (s0, s1)
    maxima = (m0, m1)
    probs = (p0, p1)
    totals = (l0, l1)
    ksv = ks.reshape(53 * 128, HD)
    vsv = vs.reshape(53 * 128, HD)

    def rows_of(part, hh, il, n):
        if n <= NS:
            at = (2 * NBD + il) * BLK
            if n > 0:
                at = at - slash[hh][n - 1] * BLK
            return part[pl.ds(pl.multiple_of(at, BLK), BLK), :]
        at = WROWS + (hh * NV + n - NS - 1) * BLK
        return part[at : at + BLK, :]

    def first(t, buf):
        for g in range(G):
            il = t * (G // 2) + g // 2
            hh = g % 2
            row = pl.multiple_of(il * BLK, BLK)
            q = q_ref[pl.ds(row, BLK), hh * HD : (hh + 1) * HD]
            m = None
            for c0 in range(0, 7, CH):
                cs = list(range(c0, min(7, c0 + CH)))
                k = jnp.concatenate([rows_of(ksv, hh, il, 2 * c + j) for c in cs for j in range(2)], axis=0)
                xx = lax.dot_general(q, k, (((1,), (1,)), ((), ())), preferred_element_type=jnp.float32)
                for c in cs:
                    x = xx[:, (c - c0) * 128 : (c - c0 + 1) * 128]
                    x = x.reshape(8, 8, 128) + bias[2 * il + hh, :, c * 128 : (c + 1) * 128][None]
                    x = x.reshape(BLK, 128)
                    if c == 0:
                        x = jnp.where(causal, x, -jnp.inf)
                    scores[buf][g, :, c * 128 : (c + 1) * 128] = x
                    m = x if m is None else jnp.maximum(m, x)
            m = jnp.max(m, axis=1, keepdims=True)
            maxima[buf][g] = jnp.broadcast_to(m, (BLK, 128))

    def second(t, buf):
        for g in range(G):
            m = maxima[buf][g]
            total = None
            for c in range(7):
                p = jnp.exp2((scores[buf][g, :, c * 128 : (c + 1) * 128] - m) * SCALE)
                total = p if total is None else total + p
                probs[buf][g, :, c * 128 : (c + 1) * 128] = p.astype(jnp.bfloat16)
            total = jnp.sum(total, axis=1, keepdims=True)
            totals[buf][g] = jnp.broadcast_to(1.0 / total, (BLK, 128))

    def third(t, buf):
        for g in range(G):
            il = t * (G // 2) + g // 2
            hh = g % 2
            row = pl.multiple_of(il * BLK, BLK)
            v = jnp.concatenate([rows_of(vsv, hh, il, n) for n in range(14)], axis=0)
            acc = jnp.dot(probs[buf][g], v, preferred_element_type=jnp.float32)
            o_ref[pl.ds(row, BLK), hh * HD : (hh + 1) * HD] = (acc * totals[buf][g]).astype(o_ref.dtype)

    steps = 2 * NBD // G
    first(0, 0)
    first(1, 1)
    second(0, 0)

    def body(u, carry):
        t = 2 * u
        for e in range(2):
            third(t + e, e)
            first(jnp.minimum(t + e + 2, steps - 1), e)
            second(jnp.minimum(t + e + 1, steps - 1), 1 - e)
        return carry

    lax.fori_loop(0, steps // 2, body, 0)


def attend(tab, q, own, swp, pas, sh2, vkv):
    hbm = pl.BlockSpec(memory_space=pl.ANY)
    smem = pl.BlockSpec(memory_space=pltpu.SMEM)
    vmem = pl.BlockSpec(memory_space=pltpu.VMEM)
    return pl.pallas_call(
        attn_kernel,
        out_shape=jax.ShapeDtypeStruct((NBD * BLK, 2 * HD), jnp.bfloat16),
        in_specs=[smem] + [hbm] * 6,
        out_specs=vmem,
        scratch_shapes=[
            pltpu.VMEM((NBD * BLK, 2 * HD), jnp.bfloat16),
            pltpu.VMEM((53, 128, HD), jnp.bfloat16),
            pltpu.VMEM((53, 128, HD), jnp.bfloat16),
            pltpu.VMEM((2 * NBD, 8, 896), jnp.float32),
            pltpu.VMEM((G, BLK, 896), jnp.float32),
            pltpu.VMEM((G, BLK, 896), jnp.float32),
            pltpu.VMEM((G, BLK, 128), jnp.float32),
            pltpu.VMEM((G, BLK, 128), jnp.float32),
            pltpu.VMEM((G, BLK, 896), jnp.bfloat16),
            pltpu.VMEM((G, BLK, 896), jnp.bfloat16),
            pltpu.VMEM((G, BLK, 128), jnp.float32),
            pltpu.VMEM((G, BLK, 128), jnp.float32),
            pltpu.SemaphoreType.DMA((7,)),
            pltpu.SemaphoreType.DMA((2,)),
        ],
        cost_estimate=pl.CostEstimate(flops=2_000_000_000, bytes_accessed=6_000_000, transcendentals=4_000_000),
        name="attend",
    )(tab, q, own, swp, pas, sh2, vkv)


def pick_kernel(tab, kv, o_ref, buf, sem):
    run = tab[0]
    picked = []
    copies = []
    for n in range(NSLOT):
        local = tab[1 + n] - run * NBD
        at = jnp.clip(local, 0, NBD - 1)
        picked.append(local == at)
        rows = pl.ds(pl.multiple_of((at & 1) * BLK, BLK), BLK)
        for part in range(2):
            copies.append(pltpu.make_async_copy(kv.at[at >> 1, part, rows], buf.at[n, part], sem.at[n, part]))
    for c in copies:
        c.start()
    for c in copies:
        c.wait()
    for n in range(NSLOT):
        ok = jnp.full((BLK, HD), jnp.where(picked[n], 1, 0), jnp.int32) == 1
        for part in range(2):
            x = buf[n, part].astype(jnp.float32)
            dst = (part * NSLOT + n) * BLK
            o_ref[dst : dst + BLK, :] = jnp.where(ok, x, 0.0).astype(jnp.bfloat16)


def pick(tab, kv):
    return pl.pallas_call(
        pick_kernel,
        out_shape=jax.ShapeDtypeStruct((NSLOT * 128, HD), jnp.bfloat16),
        in_specs=[pl.BlockSpec(memory_space=pltpu.SMEM), pl.BlockSpec(memory_space=pl.ANY)],
        out_specs=pl.BlockSpec(memory_space=pltpu.VMEM),
        scratch_shapes=[
            pltpu.VMEM((NSLOT, 2, BLK, HD), jnp.bfloat16),
            pltpu.SemaphoreType.DMA((NSLOT, 2)),
        ],
        cost_estimate=pl.CostEstimate(flops=1_000_000, bytes_accessed=1_500_000, transcendentals=0),
        name="pick",
    )(tab, kv)


def by_head(k, v):
    rows = k.shape[0]
    k3 = k.reshape(rows, KVH, HD).transpose(1, 0, 2)
    v3 = v.reshape(rows, KVH, HD).transpose(1, 0, 2)
    return jnp.repeat(jnp.stack([k3, v3], axis=1), 2, axis=0)


def exchange(x, axis):
    return lax.all_to_all(x, axis, split_axis=0, concat_axis=0, tiled=True)


def per_device(queries, key_states, value_states, vertical_blocks, slash_offsets):
    runs = lax.axis_size("qblk")
    head = lax.axis_index("head")
    run = lax.axis_index("qblk").astype(jnp.int32)
    ahead = [(r, (r + 2) % runs) for r in range(runs)]
    swap = [(r, r ^ 1) for r in range(runs)]
    mine = lambda t: lax.dynamic_slice_in_dim(t, 2 * head, 2, 0).reshape(-1)
    tab = jnp.concatenate([run.reshape(1), mine(vertical_blocks), mine(slash_offsets)])
    own = exchange(by_head(key_states, value_states), "head")
    own, tab = lax.optimization_barrier((own, tab))
    cand = pick(tab, own).reshape(runs, NSLOT * 128 // runs, HD)
    cand = exchange(cand, "qblk")
    sh2 = lax.ppermute(own, "qblk", ahead)
    swp = lax.ppermute(own, "qblk", swap)
    pas = lax.ppermute(sh2, "qblk", swap)
    part = jnp.sum(cand.astype(jnp.float32), axis=0).astype(jnp.bfloat16)
    vert = lax.all_gather(part, "qblk", axis=0, tiled=True)
    q = lax.all_to_all(queries, "head", split_axis=1, concat_axis=0, tiled=True)
    out = attend(tab, q, own, swp, pas, sh2, vert.reshape(2, NSLOT // 2, 128, HD))
    return lax.all_to_all(out, "head", split_axis=0, concat_axis=1, tiled=True)


def solution(mesh):
    spec = P(("qblk", "head"), None)
    return jax.shard_map(
        per_device,
        mesh=mesh,
        in_specs=(spec, spec, spec, P(), P()),
        out_specs=spec,
        check_vma=False,
    )
```

```python
import jax
import jax.numpy as jnp
from jax import lax
from jax.experimental import pallas as pl
from jax.experimental.pallas import tpu as pltpu
from jax.sharding import PartitionSpec as P


KVH = 8
HD = 128
BLK = 64
NV = 5
NS = 8
NBD = 32
NSLOT = 8
LOG2E = 1.4426950408889634


SCALE = (HD**-0.5) * LOG2E
WROWS = 3 * 2048
G = 4
CH = 2


def attn_kernel(
    tab, q_in, own, swp, pas, sh2, vkv, o_ref, q_ref, ks, vs, bias, s0, s1, m0, m1, p0, p1, l0, l1, sem, sem1
):
    run = tab[0]
    odd = (run & 1) == 1
    copies = [pltpu.make_async_copy(q_in, q_ref, sem.at[0])]
    for n, part in enumerate((ks, vs)):
        for m, src in ((0, sh2), (2, own)):
            copies.append(
                pltpu.make_async_copy(src.at[:, n], part.at[pl.ds(m * 16, 16)], sem.at[1 + 2 * n + m // 2])
            )
        copies.append(pltpu.make_async_copy(vkv.at[n], part.at[pl.ds(48, NSLOT // 2)], sem.at[5 + n]))
    for c in copies:
        c.start()
    for cond, src in ((odd, swp), (jnp.logical_not(odd), pas)):

        @pl.when(cond)
        def _():
            both = [
                pltpu.make_async_copy(src.at[:, n], part.at[pl.ds(16, 16)], sem1.at[n])
                for n, part in enumerate((ks, vs))
            ]
            for c in both:
                c.start()
            for c in both:
                c.wait()

    lane = lax.broadcasted_iota(jnp.int32, (8, 128), 1)
    slash = [[tab[19 + hh * NS + n] for n in range(NS)] for hh in range(2)]
    vert = [[tab[9 + hh * NV + n] for n in range(NV)] for hh in range(2)]
    spans = []
    for hh in range(2):
        named = [0] + slash[hh] + vert[hh]
        spans.append([jnp.where(lane < BLK, named[2 * c], named[2 * c + 1]) for c in range(7)])

    def mask(il, carry):
        for hh in range(2):
            for c in range(7):
                gap = run * NBD + il - spans[hh][c]
                bad = gap < 0
                if c >= 4:
                    hit = gap == 0
                    for s in slash[hh]:
                        hit = hit | (gap == s)
                    if c == 4:
                        hit = hit & (lane >= BLK)
                    bad = bad | hit
                bias[2 * il + hh, :, c * 128 : (c + 1) * 128] = jnp.where(bad, -jnp.inf, 0.0)
        return carry

    lax.fori_loop(0, NBD, mask, 0, unroll=4)
    for c in copies:
        c.wait()

    rr = lax.broadcasted_iota(jnp.int32, (BLK, 128), 0)
    cc = lax.broadcasted_iota(jnp.int32, (BLK, 128), 1)
    causal = (rr >= cc) | (cc >= BLK)
    scores = (s0, s1)
    maxima = (m0, m1)
    probs = (p0, p1)
    totals = (l0, l1)
    ksv = ks.reshape(52 * 128, HD)
    vsv = vs.reshape(52 * 128, HD)

    def rows_of(part, hh, il, n):
        if n <= NS:
            at = (2 * NBD + il) * BLK
            if n > 0:
                at = at - slash[hh][n - 1] * BLK
            return part[pl.ds(pl.multiple_of(at, BLK), BLK), :]
        slot = n - NS - 1 if hh == 0 else tab[35 + n - NS - 1]
        return part[pl.ds(pl.multiple_of(WROWS + slot * BLK, BLK), BLK), :]

    def first(t, buf):
        for g in range(G):
            il = t * (G // 2) + g // 2
            hh = g % 2
            row = pl.multiple_of(il * BLK, BLK)
            q = q_ref[pl.ds(row, BLK), hh * HD : (hh + 1) * HD]
            m = None
            for c0 in range(0, 7, CH):
                cs = list(range(c0, min(7, c0 + CH)))
                k = jnp.concatenate([rows_of(ksv, hh, il, 2 * c + j) for c in cs for j in range(2)], axis=0)
                xx = lax.dot_general(q, k, (((1,), (1,)), ((), ())), preferred_element_type=jnp.float32)
                for c in cs:
                    x = xx[:, (c - c0) * 128 : (c - c0 + 1) * 128]
                    x = x.reshape(8, 8, 128) + bias[2 * il + hh, :, c * 128 : (c + 1) * 128][None]
                    x = x.reshape(BLK, 128)
                    if c == 0:
                        x = jnp.where(causal, x, -jnp.inf)
                    scores[buf][g, :, c * 128 : (c + 1) * 128] = x
                    m = x if m is None else jnp.maximum(m, x)
            m = jnp.max(m, axis=1, keepdims=True)
            maxima[buf][g] = jnp.broadcast_to(m, (BLK, 128))

    def second(t, buf):
        for g in range(G):
            m = maxima[buf][g]
            total = None
            for c in range(7):
                p = jnp.exp2((scores[buf][g, :, c * 128 : (c + 1) * 128] - m) * SCALE)
                total = p if total is None else total + p
                probs[buf][g, :, c * 128 : (c + 1) * 128] = p.astype(jnp.bfloat16)
            total = jnp.sum(total, axis=1, keepdims=True)
            totals[buf][g] = jnp.broadcast_to(1.0 / total, (BLK, 128))

    def third(t, buf):
        for g in range(G):
            il = t * (G // 2) + g // 2
            hh = g % 2
            row = pl.multiple_of(il * BLK, BLK)
            v = jnp.concatenate([rows_of(vsv, hh, il, n) for n in range(14)], axis=0)
            acc = jnp.dot(probs[buf][g], v, preferred_element_type=jnp.float32)
            o_ref[pl.ds(row, BLK), hh * HD : (hh + 1) * HD] = (acc * totals[buf][g]).astype(o_ref.dtype)

    steps = 2 * NBD // G
    first(0, 0)
    first(1, 1)
    second(0, 0)

    def body(u, carry):
        t = 2 * u
        for e in range(2):
            third(t + e, e)
            first(jnp.minimum(t + e + 2, steps - 1), e)
            second(jnp.minimum(t + e + 1, steps - 1), 1 - e)
        return carry

    lax.fori_loop(0, steps // 2, body, 0)


def attend(tab, q, own, swp, pas, sh2, vkv):
    hbm = pl.BlockSpec(memory_space=pl.ANY)
    smem = pl.BlockSpec(memory_space=pltpu.SMEM)
    vmem = pl.BlockSpec(memory_space=pltpu.VMEM)
    return pl.pallas_call(
        attn_kernel,
        out_shape=jax.ShapeDtypeStruct((NBD * BLK, 2 * HD), jnp.bfloat16),
        in_specs=[smem] + [hbm] * 6,
        out_specs=vmem,
        scratch_shapes=[
            pltpu.VMEM((NBD * BLK, 2 * HD), jnp.bfloat16),
            pltpu.VMEM((52, 128, HD), jnp.bfloat16),
            pltpu.VMEM((52, 128, HD), jnp.bfloat16),
            pltpu.VMEM((2 * NBD, 8, 896), jnp.float32),
            pltpu.VMEM((G, BLK, 896), jnp.float32),
            pltpu.VMEM((G, BLK, 896), jnp.float32),
            pltpu.VMEM((G, BLK, 128), jnp.float32),
            pltpu.VMEM((G, BLK, 128), jnp.float32),
            pltpu.VMEM((G, BLK, 896), jnp.bfloat16),
            pltpu.VMEM((G, BLK, 896), jnp.bfloat16),
            pltpu.VMEM((G, BLK, 128), jnp.float32),
            pltpu.VMEM((G, BLK, 128), jnp.float32),
            pltpu.SemaphoreType.DMA((7,)),
            pltpu.SemaphoreType.DMA((2,)),
        ],
        cost_estimate=pl.CostEstimate(flops=2_000_000_000, bytes_accessed=6_000_000, transcendentals=4_000_000),
        name="attend",
    )(tab, q, own, swp, pas, sh2, vkv)


def pick_kernel(tab, kv, o_ref):
    run = tab[0]
    for n in range(NSLOT):
        local = tab[1 + n] - run * NBD
        at = jnp.clip(local, 0, NBD - 1)
        rows = pl.ds(pl.multiple_of((at & 1) * BLK, BLK), BLK)
        ok = jnp.full((BLK, HD), jnp.where(local == at, 1, 0), jnp.int32) == 1
        for part in range(2):
            x = kv[at >> 1, part, rows].astype(jnp.float32)
            dst = (part * NSLOT + n) * BLK
            o_ref[dst : dst + BLK, :] = jnp.where(ok, x, 0.0).astype(jnp.bfloat16)


def pick(tab, kv):
    vmem = pl.BlockSpec(memory_space=pltpu.VMEM)
    return pl.pallas_call(
        pick_kernel,
        out_shape=jax.ShapeDtypeStruct((NSLOT * 128, HD), jnp.bfloat16),
        in_specs=[pl.BlockSpec(memory_space=pltpu.SMEM), vmem],
        out_specs=vmem,
        cost_estimate=pl.CostEstimate(flops=1_000_000, bytes_accessed=1_500_000, transcendentals=0),
        name="pick",
    )(tab, kv)


def table(vertical_blocks, slash_offsets, head, run):
    vert = lax.dynamic_slice_in_dim(vertical_blocks, 2 * head, 2, 0)
    slash = lax.dynamic_slice_in_dim(slash_offsets, 2 * head, 2, 0)
    same = vert[1][:, None] == vert[0][None, :]
    fresh = jnp.logical_not(jnp.any(same, axis=1))
    n = jnp.arange(NV, dtype=jnp.int32)
    rank = jnp.sum(jnp.where((n[None, :] < n[:, None]) & fresh[None, :], 1, 0), axis=1)
    slot = jnp.where(fresh, NV + rank, jnp.sum(jnp.where(same, n[None, :], 0), axis=1))
    chosen = fresh[None, :] & (rank[None, :] == n[: NSLOT - NV, None])
    extra = jnp.sum(jnp.where(chosen, vert[1][None, :], 0), axis=1)
    parts = [run.reshape(1), vert[0], extra, vert.reshape(-1), slash.reshape(-1), slot]
    return jnp.concatenate([p.astype(jnp.int32) for p in parts])


def by_head(k, v):
    rows = k.shape[0]
    k3 = k.reshape(rows, KVH, HD).transpose(1, 0, 2)
    v3 = v.reshape(rows, KVH, HD).transpose(1, 0, 2)
    return jnp.repeat(jnp.stack([k3, v3], axis=1), 2, axis=0)


def exchange(x, axis):
    return lax.all_to_all(x, axis, split_axis=0, concat_axis=0, tiled=True)


def per_device(queries, key_states, value_states, vertical_blocks, slash_offsets):
    runs = lax.axis_size("qblk")
    head = lax.axis_index("head")
    run = lax.axis_index("qblk").astype(jnp.int32)
    ahead = [(r, (r + 2) % runs) for r in range(runs)]
    swap = [(r, r ^ 1) for r in range(runs)]
    tab = table(vertical_blocks, slash_offsets, head, run)
    own = exchange(by_head(key_states, value_states), "head")
    own, tab = lax.optimization_barrier((own, tab))
    cand = pick(tab, own).reshape(runs, NSLOT * 128 // runs, HD)
    cand = exchange(cand, "qblk")
    sh2 = lax.ppermute(own, "qblk", ahead)
    swp = lax.ppermute(own, "qblk", swap)
    pas = lax.ppermute(sh2, "qblk", swap)
    part = jnp.sum(cand.astype(jnp.float32), axis=0).astype(jnp.bfloat16)
    vert = lax.all_gather(part, "qblk", axis=0, tiled=True)
    q = lax.all_to_all(queries, "head", split_axis=1, concat_axis=0, tiled=True)
    out = attend(tab, q, own, swp, pas, sh2, vert.reshape(2, NSLOT // 2, 128, HD))
    return lax.all_to_all(out, "head", split_axis=0, concat_axis=1, tiled=True)


def solution(mesh):
    spec = P(("qblk", "head"), None)
    return jax.shard_map(
        per_device,
        mesh=mesh,
        in_specs=(spec, spec, spec, P(), P()),
        out_specs=spec,
        check_vma=False,
    )
```

```python
import jax
import jax.numpy as jnp
from jax import lax
from jax.experimental import pallas as pl
from jax.experimental.pallas import tpu as pltpu
from jax.sharding import PartitionSpec as P


KVH = 8
HD = 128
BLK = 64
NV = 5
NS = 8
NBD = 32
NSLOT = 8
LOG2E = 1.4426950408889634


SCALE = (HD**-0.5) * LOG2E
WROWS = 3 * 2048
G = 4
CH = 2


def attn_kernel(
    tab, qk2, v2, own, swp, pk, pv, vkv, o_ref, q_ref, ks, vs, bias, s0, s1, m0, m1, p0, p1, l0, l1, sem, sem1
):
    run = tab[0]
    odd = (run & 1) == 1
    copies = []
    for src, dst in (
        (qk2.at[:, 0], q_ref.at[0]),
        (qk2.at[:, 1], q_ref.at[1]),
        (qk2.at[:, 2], ks.at[pl.ds(0, 16)]),
        (v2, vs.at[pl.ds(0, 16)]),
        (own.at[:, 0], ks.at[pl.ds(32, 16)]),
        (own.at[:, 1], vs.at[pl.ds(32, 16)]),
        (vkv.at[0], ks.at[pl.ds(48, NSLOT // 2)]),
        (vkv.at[1], vs.at[pl.ds(48, NSLOT // 2)]),
    ):
        copies.append(pltpu.make_async_copy(src, dst, sem.at[len(copies)]))
    for c in copies:
        c.start()
    for cond, srcs in ((odd, (swp.at[:, 0], swp.at[:, 1])), (jnp.logical_not(odd), (pk, pv))):

        @pl.when(cond)
        def _():
            both = [
                pltpu.make_async_copy(src, part.at[pl.ds(16, 16)], sem1.at[n])
                for n, (src, part) in enumerate(zip(srcs, (ks, vs)))
            ]
            for c in both:
                c.start()
            for c in both:
                c.wait()

    lane = lax.broadcasted_iota(jnp.int32, (8, 128), 1)
    slash = [[tab[19 + hh * NS + n] for n in range(NS)] for hh in range(2)]
    vert = [[tab[9 + hh * NV + n] for n in range(NV)] for hh in range(2)]
    spans = []
    for hh in range(2):
        named = [0] + slash[hh] + vert[hh]
        spans.append([jnp.where(lane < BLK, named[2 * c], named[2 * c + 1]) for c in range(7)])

    def mask(il, carry):
        for hh in range(2):
            for c in range(7):
                gap = run * NBD + il - spans[hh][c]
                bad = gap < 0
                if c >= 4:
                    hit = gap == 0
                    for s in slash[hh]:
                        hit = hit | (gap == s)
                    if c == 4:
                        hit = hit & (lane >= BLK)
                    bad = bad | hit
                bias[2 * il + hh, :, c * 128 : (c + 1) * 128] = jnp.where(bad, -jnp.inf, 0.0)
        return carry

    lax.fori_loop(0, NBD, mask, 0, unroll=4)
    for c in copies:
        c.wait()

    rr = lax.broadcasted_iota(jnp.int32, (BLK, 128), 0)
    cc = lax.broadcasted_iota(jnp.int32, (BLK, 128), 1)
    causal = (rr >= cc) | (cc >= BLK)
    scores = (s0, s1)
    maxima = (m0, m1)
    probs = (p0, p1)
    totals = (l0, l1)
    queries = q_ref.reshape(2, NBD * BLK, HD)
    ksv = ks.reshape(52 * 128, HD)
    vsv = vs.reshape(52 * 128, HD)

    def rows_of(part, hh, il, n):
        if n <= NS:
            at = (2 * NBD + il) * BLK
            if n > 0:
                at = at - slash[hh][n - 1] * BLK
            return part[pl.ds(pl.multiple_of(at, BLK), BLK), :]
        slot = n - NS - 1 if hh == 0 else tab[35 + n - NS - 1]
        return part[pl.ds(pl.multiple_of(WROWS + slot * BLK, BLK), BLK), :]

    def first(t, buf):
        for g in range(G):
            il = t * (G // 2) + g // 2
            hh = g % 2
            row = pl.multiple_of(il * BLK, BLK)
            q = queries[hh, pl.ds(row, BLK), :]
            m = None
            for c0 in range(0, 7, CH):
                cs = list(range(c0, min(7, c0 + CH)))
                k = jnp.concatenate([rows_of(ksv, hh, il, 2 * c + j) for c in cs for j in range(2)], axis=0)
                xx = lax.dot_general(q, k, (((1,), (1,)), ((), ())), preferred_element_type=jnp.float32)
                for c in cs:
                    x = xx[:, (c - c0) * 128 : (c - c0 + 1) * 128]
                    x = x.reshape(8, 8, 128) + bias[2 * il + hh, :, c * 128 : (c + 1) * 128][None]
                    x = x.reshape(BLK, 128)
                    if c == 0:
                        x = jnp.where(causal, x, -jnp.inf)
                    scores[buf][g, :, c * 128 : (c + 1) * 128] = x
                    m = x if m is None else jnp.maximum(m, x)
            m = jnp.max(m, axis=1, keepdims=True)
            maxima[buf][g] = jnp.broadcast_to(m, (BLK, 128))

    def second(t, buf):
        for g in range(G):
            m = maxima[buf][g]
            total = None
            for c in range(7):
                p = jnp.exp2((scores[buf][g, :, c * 128 : (c + 1) * 128] - m) * SCALE)
                total = p if total is None else total + p
                probs[buf][g, :, c * 128 : (c + 1) * 128] = p.astype(jnp.bfloat16)
            total = jnp.sum(total, axis=1, keepdims=True)
            totals[buf][g] = jnp.broadcast_to(1.0 / total, (BLK, 128))

    def third(t, buf):
        for g in range(G):
            il = t * (G // 2) + g // 2
            hh = g % 2
            row = pl.multiple_of(il * BLK, BLK)
            v = jnp.concatenate([rows_of(vsv, hh, il, n) for n in range(14)], axis=0)
            acc = jnp.dot(probs[buf][g], v, preferred_element_type=jnp.float32)
            o_ref[pl.ds(row, BLK), hh * HD : (hh + 1) * HD] = (acc * totals[buf][g]).astype(o_ref.dtype)

    steps = 2 * NBD // G
    first(0, 0)
    first(1, 1)
    second(0, 0)

    def body(u, carry):
        t = 2 * u
        for e in range(2):
            third(t + e, e)
            first(jnp.minimum(t + e + 2, steps - 1), e)
            second(jnp.minimum(t + e + 1, steps - 1), 1 - e)
        return carry

    lax.fori_loop(0, steps // 2, body, 0)


def attend(tab, qk2, v2, own, swp, pk, pv, vkv):
    hbm = pl.BlockSpec(memory_space=pl.ANY)
    smem = pl.BlockSpec(memory_space=pltpu.SMEM)
    vmem = pl.BlockSpec(memory_space=pltpu.VMEM)
    return pl.pallas_call(
        attn_kernel,
        out_shape=jax.ShapeDtypeStruct((NBD * BLK, 2 * HD), jnp.bfloat16),
        in_specs=[smem] + [hbm] * 7,
        out_specs=vmem,
        scratch_shapes=[
            pltpu.VMEM((2, 16, 128, HD), jnp.bfloat16),
            pltpu.VMEM((52, 128, HD), jnp.bfloat16),
            pltpu.VMEM((52, 128, HD), jnp.bfloat16),
            pltpu.VMEM((2 * NBD, 8, 896), jnp.float32),
            pltpu.VMEM((G, BLK, 896), jnp.float32),
            pltpu.VMEM((G, BLK, 896), jnp.float32),
            pltpu.VMEM((G, BLK, 128), jnp.float32),
            pltpu.VMEM((G, BLK, 128), jnp.float32),
            pltpu.VMEM((G, BLK, 896), jnp.bfloat16),
            pltpu.VMEM((G, BLK, 896), jnp.bfloat16),
            pltpu.VMEM((G, BLK, 128), jnp.float32),
            pltpu.VMEM((G, BLK, 128), jnp.float32),
            pltpu.SemaphoreType.DMA((8,)),
            pltpu.SemaphoreType.DMA((2,)),
        ],
        cost_estimate=pl.CostEstimate(flops=2_000_000_000, bytes_accessed=6_000_000, transcendentals=4_000_000),
        name="attend",
    )(tab, qk2, v2, own, swp, pk, pv, vkv)


def pick_kernel(tab, kv, o_ref):
    run = tab[0]
    for n in range(NSLOT):
        local = tab[1 + n] - run * NBD
        at = jnp.clip(local, 0, NBD - 1)
        rows = pl.ds(pl.multiple_of((at & 1) * BLK, BLK), BLK)
        ok = jnp.full((BLK, HD), jnp.where(local == at, 1, 0), jnp.int32) == 1
        for part in range(2):
            x = kv[at >> 1, part, rows].astype(jnp.float32)
            dst = (part * NSLOT + n) * BLK
            o_ref[dst : dst + BLK, :] = jnp.where(ok, x, 0.0).astype(jnp.bfloat16)


def pick(tab, kv):
    vmem = pl.BlockSpec(memory_space=pltpu.VMEM)
    return pl.pallas_call(
        pick_kernel,
        out_shape=jax.ShapeDtypeStruct((NSLOT * 128, HD), jnp.bfloat16),
        in_specs=[pl.BlockSpec(memory_space=pltpu.SMEM), vmem],
        out_specs=vmem,
        cost_estimate=pl.CostEstimate(flops=1_000_000, bytes_accessed=1_500_000, transcendentals=0),
        name="pick",
    )(tab, kv)


def table(vertical_blocks, slash_offsets, head, run):
    vert = lax.dynamic_slice_in_dim(vertical_blocks, 2 * head, 2, 0)
    slash = lax.dynamic_slice_in_dim(slash_offsets, 2 * head, 2, 0)
    same = vert[1][:, None] == vert[0][None, :]
    fresh = jnp.logical_not(jnp.any(same, axis=1))
    n = jnp.arange(NV, dtype=jnp.int32)
    rank = jnp.sum(jnp.where((n[None, :] < n[:, None]) & fresh[None, :], 1, 0), axis=1)
    slot = jnp.where(fresh, NV + rank, jnp.sum(jnp.where(same, n[None, :], 0), axis=1))
    chosen = fresh[None, :] & (rank[None, :] == n[: NSLOT - NV, None])
    extra = jnp.sum(jnp.where(chosen, vert[1][None, :], 0), axis=1)
    parts = [run.reshape(1), vert[0], extra, vert.reshape(-1), slash.reshape(-1), slot]
    return jnp.concatenate([p.astype(jnp.int32) for p in parts])


def pack_kernel(q, k, o_ref):
    for d in range(16):
        for n in range(2):
            o_ref[d, n] = q[:, (2 * d + n) * HD : (2 * d + n + 1) * HD]
        o_ref[d, 2] = k[:, d // 2 * HD : (d // 2 + 1) * HD]


def pack(q, k):
    vmem = pl.BlockSpec(memory_space=pltpu.VMEM)
    return pl.pallas_call(
        pack_kernel,
        out_shape=jax.ShapeDtypeStruct((16, 3, 128, HD), jnp.bfloat16),
        in_specs=[vmem, vmem],
        out_specs=vmem,
        cost_estimate=pl.CostEstimate(flops=0, bytes_accessed=3_000_000, transcendentals=0),
        name="pack",
    )(q, k)


def by_head(k, v):
    rows = k.shape[0]
    k3 = k.reshape(rows, KVH, HD).transpose(1, 0, 2)
    v3 = v.reshape(rows, KVH, HD).transpose(1, 0, 2)
    return jnp.repeat(jnp.stack([k3, v3], axis=1), 2, axis=0)


def exchange(x, axis):
    return lax.all_to_all(x, axis, split_axis=0, concat_axis=0, tiled=True)


def per_device(queries, key_states, value_states, vertical_blocks, slash_offsets):
    runs = lax.axis_size("qblk")
    head = lax.axis_index("head")
    run = lax.axis_index("qblk").astype(jnp.int32)
    ahead = [(r, (r + 2) % runs) for r in range(runs)]
    swap = [(r, r ^ 1) for r in range(runs)]
    tab = table(vertical_blocks, slash_offsets, head, run)
    own = exchange(by_head(key_states, value_states), "head")
    k2 = lax.ppermute(key_states, "qblk", ahead)
    qk2 = pack(queries, k2)
    own, tab = lax.optimization_barrier((own, tab))
    cand = pick(tab, own).reshape(runs, NSLOT * 128 // runs, HD)
    cand = exchange(cand, "qblk")
    v_own = own[:, 1]
    v2 = lax.ppermute(v_own, "qblk", ahead)
    swp = lax.ppermute(own, "qblk", swap)
    pv = lax.ppermute(v2, "qblk", swap)
    part = jnp.sum(cand.astype(jnp.float32), axis=0).astype(jnp.bfloat16)
    vert = lax.all_gather(part, "qblk", axis=0, tiled=True)
    qk2 = exchange(qk2, "head")
    pk = lax.ppermute(qk2[:, 2], "qblk", swap)
    out = attend(tab, qk2, v2, own, swp, pk, pv, vert.reshape(2, NSLOT // 2, 128, HD))
    return lax.all_to_all(out, "head", split_axis=0, concat_axis=1, tiled=True)


def solution(mesh):
    spec = P(("qblk", "head"), None)
    return jax.shard_map(
        per_device,
        mesh=mesh,
        in_specs=(spec, spec, spec, P(), P()),
        out_specs=spec,
        check_vma=False,
    )
```

```python
import jax
import jax.numpy as jnp
from jax import lax
from jax.experimental import pallas as pl
from jax.experimental.pallas import tpu as pltpu
from jax.sharding import PartitionSpec as P


HD = 128
BLK = 64
NV = 5
NS = 8
NBD = 32
NSLOT = 8
LOG2E = 1.4426950408889634


SCALE = (HD**-0.5) * LOG2E
WROWS = 3 * 2048
G = 4
CH = 2


def attn_kernel(
    tab, qk2, v2, own, swp, pk, pv, vkv, o_ref, q_ref, ks, vs, bias, s0, s1, m0, m1, p0, p1, l0, l1, sem, sem1
):
    run = tab[0]
    odd = (run & 1) == 1
    copies = []
    for src, dst in (
        (qk2.at[:, 0], q_ref.at[0]),
        (qk2.at[:, 1], q_ref.at[1]),
        (qk2.at[:, 2], ks.at[pl.ds(0, 16)]),
        (v2, vs.at[pl.ds(0, 16)]),
        (own.at[:, 0], ks.at[pl.ds(32, 16)]),
        (own.at[:, 1], vs.at[pl.ds(32, 16)]),
        (vkv.at[0], ks.at[pl.ds(48, NSLOT // 2)]),
        (vkv.at[1], vs.at[pl.ds(48, NSLOT // 2)]),
    ):
        copies.append(pltpu.make_async_copy(src, dst, sem.at[len(copies)]))
    for c in copies:
        c.start()
    for cond, srcs in ((odd, (swp.at[:, 0], swp.at[:, 1])), (jnp.logical_not(odd), (pk, pv))):

        @pl.when(cond)
        def _():
            both = [
                pltpu.make_async_copy(src, part.at[pl.ds(16, 16)], sem1.at[n])
                for n, (src, part) in enumerate(zip(srcs, (ks, vs)))
            ]
            for c in both:
                c.start()

    lane = lax.broadcasted_iota(jnp.int32, (8, 128), 1)
    slash = [[tab[19 + hh * NS + n] for n in range(NS)] for hh in range(2)]
    vert = [[tab[9 + hh * NV + n] for n in range(NV)] for hh in range(2)]
    spans = []
    for hh in range(2):
        named = [0] + slash[hh] + vert[hh]
        spans.append([jnp.where(lane < BLK, named[2 * c], named[2 * c + 1]) for c in range(7)])

    def mask(il, carry):
        for hh in range(2):
            for c in range(7):
                gap = run * NBD + il - spans[hh][c]
                bad = gap < 0
                if c >= 4:
                    hit = gap == 0
                    for s in slash[hh]:
                        hit = hit | (gap == s)
                    if c == 4:
                        hit = hit & (lane >= BLK)
                    bad = bad | hit
                bias[2 * il + hh, :, c * 128 : (c + 1) * 128] = jnp.where(bad, -jnp.inf, 0.0)
        return carry

    lax.fori_loop(0, NBD, mask, 0, unroll=4)
    for c in copies:
        c.wait()
    for n, (src, part) in enumerate(((pk, ks), (pv, vs))):
        pltpu.make_async_copy(src, part.at[pl.ds(16, 16)], sem1.at[n]).wait()

    rr = lax.broadcasted_iota(jnp.int32, (BLK, 128), 0)
    cc = lax.broadcasted_iota(jnp.int32, (BLK, 128), 1)
    causal = (rr >= cc) | (cc >= BLK)
    scores = (s0, s1)
    maxima = (m0, m1)
    probs = (p0, p1)
    totals = (l0, l1)
    queries = q_ref.reshape(2, NBD * BLK, HD)
    ksv = ks.reshape(52 * 128, HD)
    vsv = vs.reshape(52 * 128, HD)

    def rows_of(part, hh, il, n):
        if n <= NS:
            at = (2 * NBD + il) * BLK
            if n > 0:
                at = at - slash[hh][n - 1] * BLK
            return part[pl.ds(pl.multiple_of(at, BLK), BLK), :]
        slot = n - NS - 1 if hh == 0 else tab[35 + n - NS - 1]
        return part[pl.ds(pl.multiple_of(WROWS + slot * BLK, BLK), BLK), :]

    def first(t, buf):
        for g in range(G):
            il = t * (G // 2) + g // 2
            hh = g % 2
            row = pl.multiple_of(il * BLK, BLK)
            q = queries[hh, pl.ds(row, BLK), :]
            m = None
            for c0 in range(0, 7, CH):
                cs = list(range(c0, min(7, c0 + CH)))
                k = jnp.concatenate([rows_of(ksv, hh, il, 2 * c + j) for c in cs for j in range(2)], axis=0)
                xx = lax.dot_general(q, k, (((1,), (1,)), ((), ())), preferred_element_type=jnp.float32)
                for c in cs:
                    x = xx[:, (c - c0) * 128 : (c - c0 + 1) * 128]
                    x = x.reshape(8, 8, 128) + bias[2 * il + hh, :, c * 128 : (c + 1) * 128][None]
                    x = x.reshape(BLK, 128)
                    if c == 0:
                        x = jnp.where(causal, x, -jnp.inf)
                    scores[buf][g, :, c * 128 : (c + 1) * 128] = x
                    m = x if m is None else jnp.maximum(m, x)
            m = jnp.max(m, axis=1, keepdims=True)
            maxima[buf][g] = jnp.broadcast_to(m, (BLK, 128))

    def second(t, buf):
        for g in range(G):
            m = maxima[buf][g]
            total = None
            for c in range(7):
                p = jnp.exp2((scores[buf][g, :, c * 128 : (c + 1) * 128] - m) * SCALE)
                total = p if total is None else total + p
                probs[buf][g, :, c * 128 : (c + 1) * 128] = p.astype(jnp.bfloat16)
            total = jnp.sum(total, axis=1, keepdims=True)
            totals[buf][g] = jnp.broadcast_to(1.0 / total, (BLK, 128))

    def third(t, buf):
        for g in range(G):
            il = t * (G // 2) + g // 2
            hh = g % 2
            row = pl.multiple_of(il * BLK, BLK)
            v = jnp.concatenate([rows_of(vsv, hh, il, n) for n in range(14)], axis=0)
            acc = jnp.dot(probs[buf][g], v, preferred_element_type=jnp.float32)
            o_ref[pl.ds(row, BLK), hh * HD : (hh + 1) * HD] = (acc * totals[buf][g]).astype(o_ref.dtype)

    steps = 2 * NBD // G
    first(0, 0)
    first(1, 1)
    second(0, 0)

    def body(u, carry):
        t = 2 * u
        for e in range(2):
            third(t + e, e)
            first(jnp.minimum(t + e + 2, steps - 1), e)
            second(jnp.minimum(t + e + 1, steps - 1), 1 - e)
        return carry

    lax.fori_loop(0, steps // 2, body, 0)


def attend(tab, qk2, v2, own, swp, pk, pv, vkv):
    hbm = pl.BlockSpec(memory_space=pl.ANY)
    smem = pl.BlockSpec(memory_space=pltpu.SMEM)
    vmem = pl.BlockSpec(memory_space=pltpu.VMEM)
    return pl.pallas_call(
        attn_kernel,
        out_shape=jax.ShapeDtypeStruct((NBD * BLK, 2 * HD), jnp.bfloat16),
        in_specs=[smem] + [hbm] * 7,
        out_specs=vmem,
        scratch_shapes=[
            pltpu.VMEM((2, 16, 128, HD), jnp.bfloat16),
            pltpu.VMEM((52, 128, HD), jnp.bfloat16),
            pltpu.VMEM((52, 128, HD), jnp.bfloat16),
            pltpu.VMEM((2 * NBD, 8, 896), jnp.float32),
            pltpu.VMEM((G, BLK, 896), jnp.float32),
            pltpu.VMEM((G, BLK, 896), jnp.float32),
            pltpu.VMEM((G, BLK, 128), jnp.float32),
            pltpu.VMEM((G, BLK, 128), jnp.float32),
            pltpu.VMEM((G, BLK, 896), jnp.bfloat16),
            pltpu.VMEM((G, BLK, 896), jnp.bfloat16),
            pltpu.VMEM((G, BLK, 128), jnp.float32),
            pltpu.VMEM((G, BLK, 128), jnp.float32),
            pltpu.SemaphoreType.DMA((8,)),
            pltpu.SemaphoreType.DMA((2,)),
        ],
        cost_estimate=pl.CostEstimate(flops=2_000_000_000, bytes_accessed=6_000_000, transcendentals=4_000_000),
        name="attend",
    )(tab, qk2, v2, own, swp, pk, pv, vkv)


def pick_kernel(tab, kv, o_ref):
    run = tab[0]
    for n in range(NSLOT):
        local = tab[1 + n] - run * NBD
        at = jnp.clip(local, 0, NBD - 1)
        rows = pl.ds(pl.multiple_of((at & 1) * BLK, BLK), BLK)
        ok = jnp.full((BLK, HD), jnp.where(local == at, 1, 0), jnp.int32) == 1
        for part in range(2):
            x = kv[at >> 1, part, rows].astype(jnp.float32)
            dst = (part * NSLOT + n) * BLK
            o_ref[dst : dst + BLK, :] = jnp.where(ok, x, 0.0).astype(jnp.bfloat16)


def pick(tab, kv):
    vmem = pl.BlockSpec(memory_space=pltpu.VMEM)
    return pl.pallas_call(
        pick_kernel,
        out_shape=jax.ShapeDtypeStruct((NSLOT * 128, HD), jnp.bfloat16),
        in_specs=[pl.BlockSpec(memory_space=pltpu.SMEM), vmem],
        out_specs=vmem,
        cost_estimate=pl.CostEstimate(flops=1_000_000, bytes_accessed=1_500_000, transcendentals=0),
        name="pick",
    )(tab, kv)


def table(vertical_blocks, slash_offsets, head, run):
    vert = lax.dynamic_slice_in_dim(vertical_blocks, 2 * head, 2, 0)
    slash = lax.dynamic_slice_in_dim(slash_offsets, 2 * head, 2, 0)
    same = vert[1][:, None] == vert[0][None, :]
    fresh = jnp.logical_not(jnp.any(same, axis=1))
    n = jnp.arange(NV, dtype=jnp.int32)
    rank = jnp.sum(jnp.where((n[None, :] < n[:, None]) & fresh[None, :], 1, 0), axis=1)
    slot = jnp.where(fresh, NV + rank, jnp.sum(jnp.where(same, n[None, :], 0), axis=1))
    chosen = fresh[None, :] & (rank[None, :] == n[: NSLOT - NV, None])
    extra = jnp.sum(jnp.where(chosen, vert[1][None, :], 0), axis=1)
    parts = [run.reshape(1), vert[0], extra, vert.reshape(-1), slash.reshape(-1), slot]
    return jnp.concatenate([p.astype(jnp.int32) for p in parts])


def pack_kernel(q, k, o_ref):
    for d in range(16):
        for n in range(2):
            o_ref[d, n] = q[:, (2 * d + n) * HD : (2 * d + n + 1) * HD]
        o_ref[d, 2] = k[:, d // 2 * HD : (d // 2 + 1) * HD]


def pack(q, k):
    vmem = pl.BlockSpec(memory_space=pltpu.VMEM)
    return pl.pallas_call(
        pack_kernel,
        out_shape=jax.ShapeDtypeStruct((16, 3, 128, HD), jnp.bfloat16),
        in_specs=[vmem, vmem],
        out_specs=vmem,
        cost_estimate=pl.CostEstimate(flops=0, bytes_accessed=3_000_000, transcendentals=0),
        name="pack",
    )(q, k)


def pair_kernel(k, v, o_ref):
    for d in range(16):
        for n, x in enumerate((k, v)):
            o_ref[d, n] = x[:, d // 2 * HD : (d // 2 + 1) * HD]


def pair(k, v):
    vmem = pl.BlockSpec(memory_space=pltpu.VMEM)
    return pl.pallas_call(
        pair_kernel,
        out_shape=jax.ShapeDtypeStruct((16, 2, 128, HD), jnp.bfloat16),
        in_specs=[vmem, vmem],
        out_specs=vmem,
        cost_estimate=pl.CostEstimate(flops=0, bytes_accessed=2_000_000, transcendentals=0),
        name="pair",
    )(k, v)


def exchange(x, axis):
    return lax.all_to_all(x, axis, split_axis=0, concat_axis=0, tiled=True)


def per_device(queries, key_states, value_states, vertical_blocks, slash_offsets):
    runs = lax.axis_size("qblk")
    head = lax.axis_index("head")
    run = lax.axis_index("qblk").astype(jnp.int32)
    ahead = [(r, (r + 2) % runs) for r in range(runs)]
    swap = [(r, r ^ 1) for r in range(runs)]
    tab = table(vertical_blocks, slash_offsets, head, run)
    kv = pair(key_states, value_states)
    own = exchange(kv, "head")
    k2 = lax.ppermute(key_states, "qblk", ahead)
    qk2 = pack(queries, k2)
    own, tab = lax.optimization_barrier((own, tab))
    cand = pick(tab, own).reshape(runs, NSLOT * 128 // runs, HD)
    cand = exchange(cand, "qblk")
    v_own = own[:, 1]
    v2 = lax.ppermute(v_own, "qblk", ahead)
    swp = lax.ppermute(own, "qblk", swap)
    pv = lax.ppermute(v2, "qblk", swap)
    part = jnp.sum(cand.astype(jnp.float32), axis=0).astype(jnp.bfloat16)
    vert = lax.all_gather(part, "qblk", axis=0, tiled=True)
    qk2 = exchange(qk2, "head")
    pk = lax.ppermute(qk2[:, 2], "qblk", swap)
    out = attend(tab, qk2, v2, own, swp, pk, pv, vert.reshape(2, NSLOT // 2, 128, HD))
    return lax.all_to_all(out, "head", split_axis=0, concat_axis=1, tiled=True)


def solution(mesh):
    spec = P(("qblk", "head"), None)
    return jax.shard_map(
        per_device,
        mesh=mesh,
        in_specs=(spec, spec, spec, P(), P()),
        out_specs=spec,
        check_vma=False,
    )
```

```python
import jax
import jax.numpy as jnp
from jax import lax
from jax.experimental import pallas as pl
from jax.experimental.pallas import tpu as pltpu
from jax.sharding import PartitionSpec as P


HD = 128
BLK = 64
NV = 5
NS = 8
NBD = 32
NSLOT = 8
LOG2E = 1.4426950408889634


SCALE = (HD**-0.5) * LOG2E
WROWS = 3 * 2048
G = 4
CH = 2


def attn_kernel(
    tab, qk2, vk2, own, swp, pk, pvk, vkv, o_ref, q_ref, ks, vs, bias, s0, s1, m0, m1, p0, p1, l0, l1, sem, sem1
):
    run = tab[0]
    odd = (run & 1) == 1
    copies = []
    for src, dst in (
        (qk2.at[:, pl.ds(0, 128)], q_ref.at[0]),
        (qk2.at[:, pl.ds(128, 128)], q_ref.at[1]),
        (qk2.at[:, pl.ds(256, BLK)], ks.at[pl.ds(0, 16), pl.ds(0, BLK)]),
        (vk2.at[:, pl.ds(128, BLK)], ks.at[pl.ds(0, 16), pl.ds(BLK, BLK)]),
        (vk2.at[:, pl.ds(0, 128)], vs.at[pl.ds(0, 16)]),
        (own.at[:, 0], ks.at[pl.ds(32, 16)]),
        (own.at[:, 1], vs.at[pl.ds(32, 16)]),
        (vkv.at[0], ks.at[pl.ds(48, NSLOT // 2)]),
        (vkv.at[1], vs.at[pl.ds(48, NSLOT // 2)]),
    ):
        copies.append(pltpu.make_async_copy(src, dst, sem.at[len(copies)]))
    for c in copies:
        c.start()

    def middle(pairs):
        return [pltpu.make_async_copy(src, dst, sem1.at[n]) for n, (src, dst) in enumerate(pairs)]

    lower = ks.at[pl.ds(16, 16), pl.ds(0, BLK)]
    upper = ks.at[pl.ds(16, 16), pl.ds(BLK, BLK)]
    values = vs.at[pl.ds(16, 16)]
    partner = middle(((pk, lower), (pvk.at[:, pl.ds(128, BLK)], upper), (pvk.at[:, pl.ds(0, 128)], values)))
    inner = middle(
        (
            (swp.at[:, 0, pl.ds(0, BLK)], lower),
            (swp.at[:, 0, pl.ds(BLK, BLK)], upper),
            (swp.at[:, 1], values),
        )
    )
    for cond, group in ((odd, inner), (jnp.logical_not(odd), partner)):

        @pl.when(cond)
        def _():
            for c in group:
                c.start()

    lane = lax.broadcasted_iota(jnp.int32, (8, 128), 1)
    slash = [[tab[19 + hh * NS + n] for n in range(NS)] for hh in range(2)]
    vert = [[tab[9 + hh * NV + n] for n in range(NV)] for hh in range(2)]
    spans = []
    for hh in range(2):
        named = [0] + slash[hh] + vert[hh]
        spans.append([jnp.where(lane < BLK, named[2 * c], named[2 * c + 1]) for c in range(7)])

    def mask(il, carry):
        for hh in range(2):
            for c in range(7):
                gap = run * NBD + il - spans[hh][c]
                bad = gap < 0
                if c >= 4:
                    hit = gap == 0
                    for s in slash[hh]:
                        hit = hit | (gap == s)
                    if c == 4:
                        hit = hit & (lane >= BLK)
                    bad = bad | hit
                bias[2 * il + hh, :, c * 128 : (c + 1) * 128] = jnp.where(bad, -jnp.inf, 0.0)
        return carry

    lax.fori_loop(0, NBD, mask, 0, unroll=4)
    for c in copies:
        c.wait()
    for c in partner:
        c.wait()

    rr = lax.broadcasted_iota(jnp.int32, (BLK, 128), 0)
    cc = lax.broadcasted_iota(jnp.int32, (BLK, 128), 1)
    causal = (rr >= cc) | (cc >= BLK)
    scores = (s0, s1)
    maxima = (m0, m1)
    probs = (p0, p1)
    totals = (l0, l1)
    queries = q_ref.reshape(2, NBD * BLK, HD)
    ksv = ks.reshape(52 * 128, HD)
    vsv = vs.reshape(52 * 128, HD)

    def rows_of(part, hh, il, n):
        if n <= NS:
            at = (2 * NBD + il) * BLK
            if n > 0:
                at = at - slash[hh][n - 1] * BLK
            return part[pl.ds(pl.multiple_of(at, BLK), BLK), :]
        slot = n - NS - 1 if hh == 0 else tab[35 + n - NS - 1]
        return part[pl.ds(pl.multiple_of(WROWS + slot * BLK, BLK), BLK), :]

    def first(t, buf):
        for g in range(G):
            il = t * (G // 2) + g // 2
            hh = g % 2
            row = pl.multiple_of(il * BLK, BLK)
            q = queries[hh, pl.ds(row, BLK), :]
            m = None
            for c0 in range(0, 7, CH):
                cs = list(range(c0, min(7, c0 + CH)))
                k = jnp.concatenate([rows_of(ksv, hh, il, 2 * c + j) for c in cs for j in range(2)], axis=0)
                xx = lax.dot_general(q, k, (((1,), (1,)), ((), ())), preferred_element_type=jnp.float32)
                for c in cs:
                    x = xx[:, (c - c0) * 128 : (c - c0 + 1) * 128]
                    x = x.reshape(8, 8, 128) + bias[2 * il + hh, :, c * 128 : (c + 1) * 128][None]
                    x = x.reshape(BLK, 128)
                    if c == 0:
                        x = jnp.where(causal, x, -jnp.inf)
                    scores[buf][g, :, c * 128 : (c + 1) * 128] = x
                    m = x if m is None else jnp.maximum(m, x)
            m = jnp.max(m, axis=1, keepdims=True)
            maxima[buf][g] = jnp.broadcast_to(m, (BLK, 128))

    def second(t, buf):
        for g in range(G):
            m = maxima[buf][g]
            total = None
            for c in range(7):
                p = jnp.exp2((scores[buf][g, :, c * 128 : (c + 1) * 128] - m) * SCALE)
                total = p if total is None else total + p
                probs[buf][g, :, c * 128 : (c + 1) * 128] = p.astype(jnp.bfloat16)
            total = jnp.sum(total, axis=1, keepdims=True)
            totals[buf][g] = jnp.broadcast_to(1.0 / total, (BLK, 128))

    def third(t, buf):
        for g in range(G):
            il = t * (G // 2) + g // 2
            hh = g % 2
            row = pl.multiple_of(il * BLK, BLK)
            v = jnp.concatenate([rows_of(vsv, hh, il, n) for n in range(14)], axis=0)
            acc = jnp.dot(probs[buf][g], v, preferred_element_type=jnp.float32)
            o_ref[pl.ds(row, BLK), hh * HD : (hh + 1) * HD] = (acc * totals[buf][g]).astype(o_ref.dtype)

    steps = 2 * NBD // G
    first(0, 0)
    first(1, 1)
    second(0, 0)

    def body(u, carry):
        t = 2 * u
        for e in range(2):
            third(t + e, e)
            first(jnp.minimum(t + e + 2, steps - 1), e)
            second(jnp.minimum(t + e + 1, steps - 1), 1 - e)
        return carry

    lax.fori_loop(0, steps // 2, body, 0)


def attend(tab, qk2, vk2, own, swp, pk, pvk, vkv):
    hbm = pl.BlockSpec(memory_space=pl.ANY)
    smem = pl.BlockSpec(memory_space=pltpu.SMEM)
    vmem = pl.BlockSpec(memory_space=pltpu.VMEM)
    return pl.pallas_call(
        attn_kernel,
        out_shape=jax.ShapeDtypeStruct((NBD * BLK, 2 * HD), jnp.bfloat16),
        in_specs=[smem] + [hbm] * 7,
        out_specs=vmem,
        scratch_shapes=[
            pltpu.VMEM((2, 16, 128, HD), jnp.bfloat16),
            pltpu.VMEM((52, 128, HD), jnp.bfloat16),
            pltpu.VMEM((52, 128, HD), jnp.bfloat16),
            pltpu.VMEM((2 * NBD, 8, 896), jnp.float32),
            pltpu.VMEM((G, BLK, 896), jnp.float32),
            pltpu.VMEM((G, BLK, 896), jnp.float32),
            pltpu.VMEM((G, BLK, 128), jnp.float32),
            pltpu.VMEM((G, BLK, 128), jnp.float32),
            pltpu.VMEM((G, BLK, 896), jnp.bfloat16),
            pltpu.VMEM((G, BLK, 896), jnp.bfloat16),
            pltpu.VMEM((G, BLK, 128), jnp.float32),
            pltpu.VMEM((G, BLK, 128), jnp.float32),
            pltpu.SemaphoreType.DMA((9,)),
            pltpu.SemaphoreType.DMA((3,)),
        ],
        cost_estimate=pl.CostEstimate(flops=2_000_000_000, bytes_accessed=6_000_000, transcendentals=4_000_000),
        name="attend",
    )(tab, qk2, vk2, own, swp, pk, pvk, vkv)


def pick_kernel(tab, kv, o_ref):
    run = tab[0]
    for n in range(NSLOT):
        local = tab[1 + n] - run * NBD
        at = jnp.clip(local, 0, NBD - 1)
        rows = pl.ds(pl.multiple_of((at & 1) * BLK, BLK), BLK)
        ok = jnp.full((BLK, HD), jnp.where(local == at, 1, 0), jnp.int32) == 1
        for part in range(2):
            x = kv[at >> 1, part, rows].astype(jnp.float32)
            dst = (part * NSLOT + n) * BLK
            o_ref[dst : dst + BLK, :] = jnp.where(ok, x, 0.0).astype(jnp.bfloat16)


def pick(tab, kv):
    vmem = pl.BlockSpec(memory_space=pltpu.VMEM)
    return pl.pallas_call(
        pick_kernel,
        out_shape=jax.ShapeDtypeStruct((NSLOT * 128, HD), jnp.bfloat16),
        in_specs=[pl.BlockSpec(memory_space=pltpu.SMEM), vmem],
        out_specs=vmem,
        cost_estimate=pl.CostEstimate(flops=1_000_000, bytes_accessed=1_500_000, transcendentals=0),
        name="pick",
    )(tab, kv)


def table(vertical_blocks, slash_offsets, head, run):
    vert = lax.dynamic_slice_in_dim(vertical_blocks, 2 * head, 2, 0)
    slash = lax.dynamic_slice_in_dim(slash_offsets, 2 * head, 2, 0)
    same = vert[1][:, None] == vert[0][None, :]
    fresh = jnp.logical_not(jnp.any(same, axis=1))
    n = jnp.arange(NV, dtype=jnp.int32)
    rank = jnp.sum(jnp.where((n[None, :] < n[:, None]) & fresh[None, :], 1, 0), axis=1)
    slot = jnp.where(fresh, NV + rank, jnp.sum(jnp.where(same, n[None, :], 0), axis=1))
    chosen = fresh[None, :] & (rank[None, :] == n[: NSLOT - NV, None])
    extra = jnp.sum(jnp.where(chosen, vert[1][None, :], 0), axis=1)
    parts = [run.reshape(1), vert[0], extra, vert.reshape(-1), slash.reshape(-1), slot]
    return jnp.concatenate([p.astype(jnp.int32) for p in parts])


def pack_kernel(q, k, o_ref):
    for d in range(16):
        for n in range(2):
            o_ref[d, n * 128 : n * 128 + 128] = q[:, (2 * d + n) * HD : (2 * d + n + 1) * HD]
        o_ref[d, 256 : 256 + BLK] = k[:, d // 2 * HD : (d // 2 + 1) * HD]


def pack(q, k):
    vmem = pl.BlockSpec(memory_space=pltpu.VMEM)
    return pl.pallas_call(
        pack_kernel,
        out_shape=jax.ShapeDtypeStruct((16, 256 + BLK, HD), jnp.bfloat16),
        in_specs=[vmem, vmem],
        out_specs=vmem,
        cost_estimate=pl.CostEstimate(flops=0, bytes_accessed=3_000_000, transcendentals=0),
        name="pack",
    )(q, k)


def pair_kernel(k, v, o_ref):
    for d in range(16):
        for n, x in enumerate((k, v)):
            o_ref[d, n] = x[:, d // 2 * HD : (d // 2 + 1) * HD]


def pair(k, v):
    vmem = pl.BlockSpec(memory_space=pltpu.VMEM)
    return pl.pallas_call(
        pair_kernel,
        out_shape=jax.ShapeDtypeStruct((16, 2, 128, HD), jnp.bfloat16),
        in_specs=[vmem, vmem],
        out_specs=vmem,
        cost_estimate=pl.CostEstimate(flops=0, bytes_accessed=2_000_000, transcendentals=0),
        name="pair",
    )(k, v)


def exchange(x, axis):
    return lax.all_to_all(x, axis, split_axis=0, concat_axis=0, tiled=True)


def per_device(queries, key_states, value_states, vertical_blocks, slash_offsets):
    runs = lax.axis_size("qblk")
    head = lax.axis_index("head")
    run = lax.axis_index("qblk").astype(jnp.int32)
    ahead = [(r, (r + 2) % runs) for r in range(runs)]
    swap = [(r, r ^ 1) for r in range(runs)]
    tab = table(vertical_blocks, slash_offsets, head, run)
    kv = pair(key_states, value_states)
    own = exchange(kv, "head")
    k2 = lax.ppermute(key_states[:BLK], "qblk", ahead)
    qk2 = pack(queries, k2)
    own, tab = lax.optimization_barrier((own, tab))
    cand = pick(tab, own).reshape(runs, NSLOT * 128 // runs, HD)
    cand = exchange(cand, "qblk")
    vk_own = jnp.concatenate([own[:, 1], own[:, 0, BLK:]], axis=1)
    vk2 = lax.ppermute(vk_own, "qblk", ahead)
    swp = lax.ppermute(own, "qblk", swap)
    pvk = lax.ppermute(vk2, "qblk", swap)
    part = jnp.sum(cand.astype(jnp.float32), axis=0).astype(jnp.bfloat16)
    vert = lax.all_gather(part, "qblk", axis=0, tiled=True)
    qk2 = exchange(qk2, "head")
    pk = lax.ppermute(qk2[:, 256:], "qblk", swap)
    out = attend(tab, qk2, vk2, own, swp, pk, pvk, vert.reshape(2, NSLOT // 2, 128, HD))
    return lax.all_to_all(out, "head", split_axis=0, concat_axis=1, tiled=True)


def solution(mesh):
    spec = P(("qblk", "head"), None)
    return jax.shard_map(
        per_device,
        mesh=mesh,
        in_specs=(spec, spec, spec, P(), P()),
        out_specs=spec,
        check_vma=False,
    )
```

```python
import jax
import jax.numpy as jnp
from jax import lax
from jax.experimental import pallas as pl
from jax.experimental.pallas import tpu as pltpu
from jax.sharding import PartitionSpec as P


HD = 128
BLK = 64
NV = 5
NS = 8
NBD = 32
NSLOT = 8
LOG2E = 1.4426950408889634


SCALE = (HD**-0.5) * LOG2E
WROWS = 3 * 2048
G = 4
CH = 2


def attn_kernel(
    tab, qk2, vk2, own, swp, pk, pvk, vkv, o_ref, q_ref, ks, vs, bias, s0, s1, m0, m1, p0, p1, l0, l1, sem, sem1
):
    run = tab[0]
    odd = (run & 1) == 1
    copies = []
    for src, dst in (
        (qk2.at[:, pl.ds(0, 128)], q_ref.at[0]),
        (qk2.at[:, pl.ds(128, 128)], q_ref.at[1]),
        (qk2.at[:, pl.ds(256, BLK)], ks.at[pl.ds(0, 16), pl.ds(0, BLK)]),
        (vk2.at[:, pl.ds(128, BLK)], ks.at[pl.ds(0, 16), pl.ds(BLK, BLK)]),
        (vk2.at[:, pl.ds(0, 128)], vs.at[pl.ds(0, 16)]),
        (own.at[:, 0], ks.at[pl.ds(32, 16)]),
        (own.at[:, 1], vs.at[pl.ds(32, 16)]),
        (vkv.at[0], ks.at[pl.ds(48, NSLOT // 2)]),
        (vkv.at[1], vs.at[pl.ds(48, NSLOT // 2)]),
    ):
        copies.append(pltpu.make_async_copy(src, dst, sem.at[len(copies)]))
    for c in copies:
        c.start()

    def middle(pairs):
        return [pltpu.make_async_copy(src, dst, sem1.at[n]) for n, (src, dst) in enumerate(pairs)]

    lower = ks.at[pl.ds(16, 16), pl.ds(0, BLK)]
    upper = ks.at[pl.ds(16, 16), pl.ds(BLK, BLK)]
    values = vs.at[pl.ds(16, 16)]
    partner = middle(((pk, lower), (pvk.at[:, pl.ds(128, BLK)], upper), (pvk.at[:, pl.ds(0, 128)], values)))
    inner = middle(
        (
            (swp.at[:, 0, pl.ds(0, BLK)], lower),
            (swp.at[:, 0, pl.ds(BLK, BLK)], upper),
            (swp.at[:, 1], values),
        )
    )
    for cond, group in ((odd, inner), (jnp.logical_not(odd), partner)):

        @pl.when(cond)
        def _():
            for c in group:
                c.start()

    lane = lax.broadcasted_iota(jnp.int32, (8, 128), 1)
    slash = [[tab[19 + hh * NS + n] for n in range(NS)] for hh in range(2)]
    vert = [[tab[9 + hh * NV + n] for n in range(NV)] for hh in range(2)]
    spans = []
    for hh in range(2):
        named = [0] + slash[hh] + vert[hh]
        spans.append([jnp.where(lane < BLK, named[2 * c], named[2 * c + 1]) for c in range(7)])

    def mask(il, carry):
        for hh in range(2):
            for c in range(7):
                gap = run * NBD + il - spans[hh][c]
                bad = gap < 0
                if c >= 4:
                    hit = gap == 0
                    for s in slash[hh]:
                        hit = hit | (gap == s)
                    if c == 4:
                        hit = hit & (lane >= BLK)
                    bad = bad | hit
                bias[2 * il + hh, :, c * 128 : (c + 1) * 128] = jnp.where(bad, -jnp.inf, 0.0)
        return carry

    lax.fori_loop(0, NBD, mask, 0, unroll=4)
    for c in copies:
        c.wait()
    for c in partner:
        c.wait()

    rr = lax.broadcasted_iota(jnp.int32, (BLK, 128), 0)
    cc = lax.broadcasted_iota(jnp.int32, (BLK, 128), 1)
    causal = (rr >= cc) | (cc >= BLK)
    scores = (s0, s1)
    maxima = (m0, m1)
    probs = (p0, p1)
    totals = (l0, l1)
    queries = q_ref.reshape(2, NBD * BLK, HD)
    ksv = ks.reshape(52 * 128, HD)
    vsv = vs.reshape(52 * 128, HD)

    def rows_of(part, hh, il, n):
        if n <= NS:
            at = (2 * NBD + il) * BLK
            if n > 0:
                at = at - slash[hh][n - 1] * BLK
            return part[pl.ds(pl.multiple_of(at, BLK), BLK), :]
        slot = n - NS - 1 if hh == 0 else tab[35 + n - NS - 1]
        return part[pl.ds(pl.multiple_of(WROWS + slot * BLK, BLK), BLK), :]

    def first(t, buf):
        for g in range(G):
            il = t * (G // 2) + g // 2
            hh = g % 2
            row = pl.multiple_of(il * BLK, BLK)
            q = queries[hh, pl.ds(row, BLK), :]
            m = None
            for c0 in range(0, 7, CH):
                cs = list(range(c0, min(7, c0 + CH)))
                k = jnp.concatenate([rows_of(ksv, hh, il, 2 * c + j) for c in cs for j in range(2)], axis=0)
                xx = lax.dot_general(q, k, (((1,), (1,)), ((), ())), preferred_element_type=jnp.float32)
                for c in cs:
                    x = xx[:, (c - c0) * 128 : (c - c0 + 1) * 128]
                    x = x.reshape(8, 8, 128) + bias[2 * il + hh, :, c * 128 : (c + 1) * 128][None]
                    x = x.reshape(BLK, 128)
                    if c == 0:
                        x = jnp.where(causal, x, -jnp.inf)
                    scores[buf][g, :, c * 128 : (c + 1) * 128] = x
                    m = x if m is None else jnp.maximum(m, x)
            m = jnp.max(m, axis=1, keepdims=True)
            maxima[buf][g] = jnp.broadcast_to(m, (BLK, 128))

    def second(t, buf):
        for g in range(G):
            m = maxima[buf][g]
            total = None
            for c in range(7):
                p = jnp.exp2((scores[buf][g, :, c * 128 : (c + 1) * 128] - m) * SCALE)
                total = p if total is None else total + p
                probs[buf][g, :, c * 128 : (c + 1) * 128] = p.astype(jnp.bfloat16)
            total = jnp.sum(total, axis=1, keepdims=True)
            totals[buf][g] = jnp.broadcast_to(1.0 / total, (BLK, 128))

    def third(t, buf):
        for g in range(G):
            il = t * (G // 2) + g // 2
            hh = g % 2
            row = pl.multiple_of(il * BLK, BLK)
            v = jnp.concatenate([rows_of(vsv, hh, il, n) for n in range(14)], axis=0)
            acc = jnp.dot(probs[buf][g], v, preferred_element_type=jnp.float32)
            o_ref[pl.ds(row, BLK), hh * HD : (hh + 1) * HD] = (acc * totals[buf][g]).astype(o_ref.dtype)

    steps = 2 * NBD // G
    first(0, 0)
    first(1, 1)
    second(0, 0)

    def body(u, carry):
        t = 2 * u
        for e in range(2):
            third(t + e, e)
            first(jnp.minimum(t + e + 2, steps - 1), e)
            second(jnp.minimum(t + e + 1, steps - 1), 1 - e)
        return carry

    lax.fori_loop(0, steps // 2, body, 0)


def attend(tab, qk2, vk2, own, swp, pk, pvk, vkv):
    hbm = pl.BlockSpec(memory_space=pl.ANY)
    smem = pl.BlockSpec(memory_space=pltpu.SMEM)
    vmem = pl.BlockSpec(memory_space=pltpu.VMEM)
    return pl.pallas_call(
        attn_kernel,
        out_shape=jax.ShapeDtypeStruct((NBD * BLK, 2 * HD), jnp.bfloat16),
        in_specs=[smem] + [hbm] * 7,
        out_specs=vmem,
        scratch_shapes=[
            pltpu.VMEM((2, 16, 128, HD), jnp.bfloat16),
            pltpu.VMEM((52, 128, HD), jnp.bfloat16),
            pltpu.VMEM((52, 128, HD), jnp.bfloat16),
            pltpu.VMEM((2 * NBD, 8, 896), jnp.float32),
            pltpu.VMEM((G, BLK, 896), jnp.float32),
            pltpu.VMEM((G, BLK, 896), jnp.float32),
            pltpu.VMEM((G, BLK, 128), jnp.float32),
            pltpu.VMEM((G, BLK, 128), jnp.float32),
            pltpu.VMEM((G, BLK, 896), jnp.bfloat16),
            pltpu.VMEM((G, BLK, 896), jnp.bfloat16),
            pltpu.VMEM((G, BLK, 128), jnp.float32),
            pltpu.VMEM((G, BLK, 128), jnp.float32),
            pltpu.SemaphoreType.DMA((9,)),
            pltpu.SemaphoreType.DMA((3,)),
        ],
        cost_estimate=pl.CostEstimate(flops=2_000_000_000, bytes_accessed=6_000_000, transcendentals=4_000_000),
        name="attend",
    )(tab, qk2, vk2, own, swp, pk, pvk, vkv)


def pick_kernel(tab, kv, o_ref):
    run = tab[0]
    for n in range(NSLOT):
        local = tab[1 + n] - run * NBD
        at = jnp.clip(local, 0, NBD - 1)
        rows = pl.ds(pl.multiple_of((at & 1) * BLK, BLK), BLK)
        ok = jnp.full((BLK, HD), jnp.where(local == at, 1, 0), jnp.int32) == 1
        for part in range(2):
            x = kv[at >> 1, part, rows].astype(jnp.float32)
            dst = (part * NSLOT + n) * BLK
            o_ref[dst : dst + BLK, :] = jnp.where(ok, x, 0.0).astype(jnp.bfloat16)


def pick(tab, kv):
    vmem = pl.BlockSpec(memory_space=pltpu.VMEM)
    return pl.pallas_call(
        pick_kernel,
        out_shape=jax.ShapeDtypeStruct((NSLOT * 128, HD), jnp.bfloat16),
        in_specs=[pl.BlockSpec(memory_space=pltpu.SMEM), vmem],
        out_specs=vmem,
        cost_estimate=pl.CostEstimate(flops=1_000_000, bytes_accessed=1_500_000, transcendentals=0),
        name="pick",
    )(tab, kv)


def table(vertical_blocks, slash_offsets, head, run):
    vert = lax.dynamic_slice_in_dim(vertical_blocks, 2 * head, 2, 0)
    slash = lax.dynamic_slice_in_dim(slash_offsets, 2 * head, 2, 0)
    same = vert[1][:, None] == vert[0][None, :]
    fresh = jnp.logical_not(jnp.any(same, axis=1))
    n = jnp.arange(NV, dtype=jnp.int32)
    rank = jnp.sum(jnp.where((n[None, :] < n[:, None]) & fresh[None, :], 1, 0), axis=1)
    slot = jnp.where(fresh, NV + rank, jnp.sum(jnp.where(same, n[None, :], 0), axis=1))
    chosen = fresh[None, :] & (rank[None, :] == n[: NSLOT - NV, None])
    extra = jnp.sum(jnp.where(chosen, vert[1][None, :], 0), axis=1)
    parts = [run.reshape(1), vert[0], extra, vert.reshape(-1), slash.reshape(-1), slot]
    return jnp.concatenate([p.astype(jnp.int32) for p in parts])


def pack_kernel(q, k, o_ref):
    for d in range(16):
        for n in range(2):
            o_ref[d, n * 128 : n * 128 + 128] = q[:, (2 * d + n) * HD : (2 * d + n + 1) * HD]
        o_ref[d, 256 : 256 + BLK] = k[:, d // 2 * HD : (d // 2 + 1) * HD]


def pack(q, k):
    vmem = pl.BlockSpec(memory_space=pltpu.VMEM)
    return pl.pallas_call(
        pack_kernel,
        out_shape=jax.ShapeDtypeStruct((16, 256 + BLK, HD), jnp.bfloat16),
        in_specs=[vmem, vmem],
        out_specs=vmem,
        cost_estimate=pl.CostEstimate(flops=0, bytes_accessed=3_000_000, transcendentals=0),
        name="pack",
    )(q, k)


def pair_kernel(k, v, o_ref):
    for d in range(4):
        for n, x in enumerate((k, v)):
            o_ref[d, n] = x[:, d // 2 * HD : (d // 2 + 1) * HD]


def pair(k, v):
    tile = pl.BlockSpec((128, 2 * HD), lambda i: (0, i))
    return pl.pallas_call(
        pair_kernel,
        grid=(4,),
        out_shape=jax.ShapeDtypeStruct((16, 2, 128, HD), jnp.bfloat16),
        in_specs=[tile, tile],
        out_specs=pl.BlockSpec((4, 2, 128, HD), lambda i: (i, 0, 0, 0)),
        cost_estimate=pl.CostEstimate(flops=0, bytes_accessed=2_000_000, transcendentals=0),
        name="pair",
    )(k, v)


def exchange(x, axis):
    return lax.all_to_all(x, axis, split_axis=0, concat_axis=0, tiled=True)


def per_device(queries, key_states, value_states, vertical_blocks, slash_offsets):
    runs = lax.axis_size("qblk")
    head = lax.axis_index("head")
    run = lax.axis_index("qblk").astype(jnp.int32)
    ahead = [(r, (r + 2) % runs) for r in range(runs)]
    swap = [(r, r ^ 1) for r in range(runs)]
    tab = table(vertical_blocks, slash_offsets, head, run)
    kv = pair(key_states, value_states)
    own = exchange(kv, "head")
    k2 = lax.ppermute(key_states[:BLK], "qblk", ahead)
    qk2 = pack(queries, k2)
    own, tab = lax.optimization_barrier((own, tab))
    cand = pick(tab, own).reshape(runs, NSLOT * 128 // runs, HD)
    cand = exchange(cand, "qblk")
    vk_own = jnp.concatenate([own[:, 1], own[:, 0, BLK:]], axis=1)
    vk2 = lax.ppermute(vk_own, "qblk", ahead)
    swp = lax.ppermute(own, "qblk", swap)
    pvk = lax.ppermute(vk2, "qblk", swap)
    part = jnp.sum(cand.astype(jnp.float32), axis=0).astype(jnp.bfloat16)
    vert = lax.all_gather(part, "qblk", axis=0, tiled=True)
    qk2 = exchange(qk2, "head")
    pk = lax.ppermute(qk2[:, 256:], "qblk", swap)
    out = attend(tab, qk2, vk2, own, swp, pk, pvk, vert.reshape(2, NSLOT // 2, 128, HD))
    return lax.all_to_all(out, "head", split_axis=0, concat_axis=1, tiled=True)


def solution(mesh):
    spec = P(("qblk", "head"), None)
    return jax.shard_map(
        per_device,
        mesh=mesh,
        in_specs=(spec, spec, spec, P(), P()),
        out_specs=spec,
        check_vma=False,
    )
```

```python
import jax
import jax.numpy as jnp
from jax import lax
from jax.experimental import pallas as pl
from jax.experimental.pallas import tpu as pltpu
from jax.sharding import PartitionSpec as P


HD = 128
BLK = 64
NV = 5
NS = 8
NBD = 32
NSLOT = 8
CUT = 96
LOG2E = 1.4426950408889634


SCALE = (HD**-0.5) * LOG2E
WROWS = 3 * 2048
G = 4
CH = 2


def attn_kernel(
    tab, qk2, vk2, own, swp, pk, pvk, vkv, o_ref, q_ref, ks, vs, bias, s0, s1, m0, m1, p0, p1, l0, l1, sem, sem1
):
    run = tab[0]
    odd = (run & 1) == 1
    copies = []
    for src, dst in (
        (qk2.at[:, pl.ds(0, 128)], q_ref.at[0]),
        (qk2.at[:, pl.ds(128, 128)], q_ref.at[1]),
        (qk2.at[:, pl.ds(256, CUT)], ks.at[pl.ds(0, 16), pl.ds(0, CUT)]),
        (vk2.at[:, pl.ds(128, 128 - CUT)], ks.at[pl.ds(0, 16), pl.ds(CUT, 128 - CUT)]),
        (vk2.at[:, pl.ds(0, 128)], vs.at[pl.ds(0, 16)]),
        (own.at[:, 0], ks.at[pl.ds(32, 16)]),
        (own.at[:, 1], vs.at[pl.ds(32, 16)]),
        (vkv.at[0], ks.at[pl.ds(48, NSLOT // 2)]),
        (vkv.at[1], vs.at[pl.ds(48, NSLOT // 2)]),
    ):
        copies.append(pltpu.make_async_copy(src, dst, sem.at[len(copies)]))
    for c in copies:
        c.start()

    def middle(pairs):
        return [pltpu.make_async_copy(src, dst, sem1.at[n]) for n, (src, dst) in enumerate(pairs)]

    lower = ks.at[pl.ds(16, 16), pl.ds(0, CUT)]
    upper = ks.at[pl.ds(16, 16), pl.ds(CUT, 128 - CUT)]
    values = vs.at[pl.ds(16, 16)]
    partner = middle(((pk, lower), (pvk.at[:, pl.ds(128, 128 - CUT)], upper), (pvk.at[:, pl.ds(0, 128)], values)))
    inner = middle(
        (
            (swp.at[:, 0, pl.ds(0, CUT)], lower),
            (swp.at[:, 0, pl.ds(CUT, 128 - CUT)], upper),
            (swp.at[:, 1], values),
        )
    )
    for cond, group in ((odd, inner), (jnp.logical_not(odd), partner)):

        @pl.when(cond)
        def _():
            for c in group:
                c.start()

    lane = lax.broadcasted_iota(jnp.int32, (8, 128), 1)
    slash = [[tab[19 + hh * NS + n] for n in range(NS)] for hh in range(2)]
    vert = [[tab[9 + hh * NV + n] for n in range(NV)] for hh in range(2)]
    spans = []
    for hh in range(2):
        named = [0] + slash[hh] + vert[hh]
        spans.append([jnp.where(lane < BLK, named[2 * c], named[2 * c + 1]) for c in range(7)])

    def mask(il, carry):
        for hh in range(2):
            for c in range(7):
                gap = run * NBD + il - spans[hh][c]
                bad = gap < 0
                if c >= 4:
                    hit = gap == 0
                    for s in slash[hh]:
                        hit = hit | (gap == s)
                    if c == 4:
                        hit = hit & (lane >= BLK)
                    bad = bad | hit
                bias[2 * il + hh, :, c * 128 : (c + 1) * 128] = jnp.where(bad, -jnp.inf, 0.0)
        return carry

    lax.fori_loop(0, NBD, mask, 0, unroll=4)
    for c in copies:
        c.wait()
    for c in partner:
        c.wait()

    rr = lax.broadcasted_iota(jnp.int32, (BLK, 128), 0)
    cc = lax.broadcasted_iota(jnp.int32, (BLK, 128), 1)
    causal = (rr >= cc) | (cc >= BLK)
    scores = (s0, s1)
    maxima = (m0, m1)
    probs = (p0, p1)
    totals = (l0, l1)
    queries = q_ref.reshape(2, NBD * BLK, HD)
    ksv = ks.reshape(52 * 128, HD)
    vsv = vs.reshape(52 * 128, HD)

    def rows_of(part, hh, il, n):
        if n <= NS:
            at = (2 * NBD + il) * BLK
            if n > 0:
                at = at - slash[hh][n - 1] * BLK
            return part[pl.ds(pl.multiple_of(at, BLK), BLK), :]
        slot = n - NS - 1 if hh == 0 else tab[35 + n - NS - 1]
        return part[pl.ds(pl.multiple_of(WROWS + slot * BLK, BLK), BLK), :]

    def first(t, buf):
        for g in range(G):
            il = t * (G // 2) + g // 2
            hh = g % 2
            row = pl.multiple_of(il * BLK, BLK)
            q = queries[hh, pl.ds(row, BLK), :]
            m = None
            for c0 in range(0, 7, CH):
                cs = list(range(c0, min(7, c0 + CH)))
                k = jnp.concatenate([rows_of(ksv, hh, il, 2 * c + j) for c in cs for j in range(2)], axis=0)
                xx = lax.dot_general(q, k, (((1,), (1,)), ((), ())), preferred_element_type=jnp.float32)
                for c in cs:
                    x = xx[:, (c - c0) * 128 : (c - c0 + 1) * 128]
                    x = x.reshape(8, 8, 128) + bias[2 * il + hh, :, c * 128 : (c + 1) * 128][None]
                    x = x.reshape(BLK, 128)
                    if c == 0:
                        x = jnp.where(causal, x, -jnp.inf)
                    scores[buf][g, :, c * 128 : (c + 1) * 128] = x
                    m = x if m is None else jnp.maximum(m, x)
            m = jnp.max(m, axis=1, keepdims=True)
            maxima[buf][g] = jnp.broadcast_to(m, (BLK, 128))

    def second(t, buf):
        for g in range(G):
            m = maxima[buf][g]
            total = None
            for c in range(7):
                p = jnp.exp2((scores[buf][g, :, c * 128 : (c + 1) * 128] - m) * SCALE)
                total = p if total is None else total + p
                probs[buf][g, :, c * 128 : (c + 1) * 128] = p.astype(jnp.bfloat16)
            total = jnp.sum(total, axis=1, keepdims=True)
            totals[buf][g] = jnp.broadcast_to(1.0 / total, (BLK, 128))

    def third(t, buf):
        for g in range(G):
            il = t * (G // 2) + g // 2
            hh = g % 2
            row = pl.multiple_of(il * BLK, BLK)
            v = jnp.concatenate([rows_of(vsv, hh, il, n) for n in range(14)], axis=0)
            acc = jnp.dot(probs[buf][g], v, preferred_element_type=jnp.float32)
            o_ref[pl.ds(row, BLK), hh * HD : (hh + 1) * HD] = (acc * totals[buf][g]).astype(o_ref.dtype)

    steps = 2 * NBD // G
    first(0, 0)
    first(1, 1)
    second(0, 0)

    def body(u, carry):
        t = 2 * u
        for e in range(2):
            third(t + e, e)
            first(jnp.minimum(t + e + 2, steps - 1), e)
            second(jnp.minimum(t + e + 1, steps - 1), 1 - e)
        return carry

    lax.fori_loop(0, steps // 2, body, 0)


def attend(tab, qk2, vk2, own, swp, pk, pvk, vkv):
    hbm = pl.BlockSpec(memory_space=pl.ANY)
    smem = pl.BlockSpec(memory_space=pltpu.SMEM)
    vmem = pl.BlockSpec(memory_space=pltpu.VMEM)
    return pl.pallas_call(
        attn_kernel,
        out_shape=jax.ShapeDtypeStruct((NBD * BLK, 2 * HD), jnp.bfloat16),
        in_specs=[smem] + [hbm] * 7,
        out_specs=vmem,
        scratch_shapes=[
            pltpu.VMEM((2, 16, 128, HD), jnp.bfloat16),
            pltpu.VMEM((52, 128, HD), jnp.bfloat16),
            pltpu.VMEM((52, 128, HD), jnp.bfloat16),
            pltpu.VMEM((2 * NBD, 8, 896), jnp.float32),
            pltpu.VMEM((G, BLK, 896), jnp.float32),
            pltpu.VMEM((G, BLK, 896), jnp.float32),
            pltpu.VMEM((G, BLK, 128), jnp.float32),
            pltpu.VMEM((G, BLK, 128), jnp.float32),
            pltpu.VMEM((G, BLK, 896), jnp.bfloat16),
            pltpu.VMEM((G, BLK, 896), jnp.bfloat16),
            pltpu.VMEM((G, BLK, 128), jnp.float32),
            pltpu.VMEM((G, BLK, 128), jnp.float32),
            pltpu.SemaphoreType.DMA((9,)),
            pltpu.SemaphoreType.DMA((3,)),
        ],
        cost_estimate=pl.CostEstimate(flops=2_000_000_000, bytes_accessed=6_000_000, transcendentals=4_000_000),
        name="attend",
    )(tab, qk2, vk2, own, swp, pk, pvk, vkv)


def pick_kernel(tab, kv, o_ref):
    run = tab[0]
    for n in range(NSLOT):
        local = tab[1 + n] - run * NBD
        at = jnp.clip(local, 0, NBD - 1)
        rows = pl.ds(pl.multiple_of((at & 1) * BLK, BLK), BLK)
        ok = jnp.full((BLK, HD), jnp.where(local == at, 1, 0), jnp.int32) == 1
        for part in range(2):
            x = kv[at >> 1, part, rows].astype(jnp.float32)
            dst = (part * NSLOT + n) * BLK
            o_ref[dst : dst + BLK, :] = jnp.where(ok, x, 0.0).astype(jnp.bfloat16)


def pick(tab, kv):
    vmem = pl.BlockSpec(memory_space=pltpu.VMEM)
    return pl.pallas_call(
        pick_kernel,
        out_shape=jax.ShapeDtypeStruct((NSLOT * 128, HD), jnp.bfloat16),
        in_specs=[pl.BlockSpec(memory_space=pltpu.SMEM), vmem],
        out_specs=vmem,
        cost_estimate=pl.CostEstimate(flops=1_000_000, bytes_accessed=1_500_000, transcendentals=0),
        name="pick",
    )(tab, kv)


def table(vertical_blocks, slash_offsets, head, run):
    vert = lax.dynamic_slice_in_dim(vertical_blocks, 2 * head, 2, 0)
    slash = lax.dynamic_slice_in_dim(slash_offsets, 2 * head, 2, 0)
    same = vert[1][:, None] == vert[0][None, :]
    fresh = jnp.logical_not(jnp.any(same, axis=1))
    n = jnp.arange(NV, dtype=jnp.int32)
    rank = jnp.sum(jnp.where((n[None, :] < n[:, None]) & fresh[None, :], 1, 0), axis=1)
    slot = jnp.where(fresh, NV + rank, jnp.sum(jnp.where(same, n[None, :], 0), axis=1))
    chosen = fresh[None, :] & (rank[None, :] == n[: NSLOT - NV, None])
    extra = jnp.sum(jnp.where(chosen, vert[1][None, :], 0), axis=1)
    parts = [run.reshape(1), vert[0], extra, vert.reshape(-1), slash.reshape(-1), slot]
    return jnp.concatenate([p.astype(jnp.int32) for p in parts])


def pack_kernel(q, k, o_ref):
    for d in range(16):
        for n in range(2):
            o_ref[d, n * 128 : n * 128 + 128] = q[:, (2 * d + n) * HD : (2 * d + n + 1) * HD]
        o_ref[d, 256 : 256 + CUT] = k[:, d // 2 * HD : (d // 2 + 1) * HD]


def pack(q, k):
    vmem = pl.BlockSpec(memory_space=pltpu.VMEM)
    return pl.pallas_call(
        pack_kernel,
        out_shape=jax.ShapeDtypeStruct((16, 256 + CUT, HD), jnp.bfloat16),
        in_specs=[vmem, vmem],
        out_specs=vmem,
        cost_estimate=pl.CostEstimate(flops=0, bytes_accessed=3_000_000, transcendentals=0),
        name="pack",
    )(q, k)


def pair_kernel(k, v, o_ref):
    for d in range(16):
        for n, x in enumerate((k, v)):
            o_ref[d, n] = x[:, d // 2 * HD : (d // 2 + 1) * HD]


def pair(k, v):
    vmem = pl.BlockSpec(memory_space=pltpu.VMEM)
    return pl.pallas_call(
        pair_kernel,
        out_shape=jax.ShapeDtypeStruct((16, 2, 128, HD), jnp.bfloat16),
        in_specs=[vmem, vmem],
        out_specs=vmem,
        cost_estimate=pl.CostEstimate(flops=0, bytes_accessed=2_000_000, transcendentals=0),
        name="pair",
    )(k, v)


def exchange(x, axis):
    return lax.all_to_all(x, axis, split_axis=0, concat_axis=0, tiled=True)


def per_device(queries, key_states, value_states, vertical_blocks, slash_offsets):
    runs = lax.axis_size("qblk")
    head = lax.axis_index("head")
    run = lax.axis_index("qblk").astype(jnp.int32)
    ahead = [(r, (r + 2) % runs) for r in range(runs)]
    swap = [(r, r ^ 1) for r in range(runs)]
    tab = table(vertical_blocks, slash_offsets, head, run)
    kv = pair(key_states, value_states)
    own = exchange(kv, "head")
    k2 = lax.ppermute(key_states[:CUT], "qblk", ahead)
    qk2 = pack(queries, k2)
    own, tab = lax.optimization_barrier((own, tab))
    cand = pick(tab, own).reshape(runs, NSLOT * 128 // runs, HD)
    cand = exchange(cand, "qblk")
    vk_own = jnp.concatenate([own[:, 1], own[:, 0, CUT:]], axis=1)
    vk2 = lax.ppermute(vk_own, "qblk", ahead)
    swp = lax.ppermute(own, "qblk", swap)
    pvk = lax.ppermute(vk2, "qblk", swap)
    part = jnp.sum(cand.astype(jnp.float32), axis=0).astype(jnp.bfloat16)
    vert = lax.all_gather(part, "qblk", axis=0, tiled=True)
    qk2 = exchange(qk2, "head")
    pk = lax.ppermute(qk2[:, 256:], "qblk", swap)
    out = attend(tab, qk2, vk2, own, swp, pk, pvk, vert.reshape(2, NSLOT // 2, 128, HD))
    return lax.all_to_all(out, "head", split_axis=0, concat_axis=1, tiled=True)


def solution(mesh):
    spec = P(("qblk", "head"), None)
    return jax.shard_map(
        per_device,
        mesh=mesh,
        in_specs=(spec, spec, spec, P(), P()),
        out_specs=spec,
        check_vma=False,
    )
```
